128 devices in a mesh: sta: 16 (over x, z_lo, core), win: 8 (over z_hi, y).
Axes of the slice: x: 4, y: 4, z: 4 (z_hi: 2, z_lo: 2; z = z_hi * 2 + z_lo), core: 2. Of those that a mesh axis runs over, the one named last changes fastest.
Arguments:
- traces: float32 [128, 128, 2048], P('sta', 'win'), may hold values from -24 to 24
- gap_mask: int32 [128, 128], P('sta', 'win'), may hold values 0 or 1
- pair_mask: int32 [128, 5, 8], P('sta'), may hold values from 0 to 1, as said below
Outputs:
- pws: float32 [128, 5, 8, 512], P('sta', None, None, 'win')
The draws below stay inside these ranges and needn't reach their ends.
Inputs may be any that keep to these rules, and one draw needn't show every extreme that they name: pair_mask is 0 for a station paired with itself (offset index 2, same station of the block).
All inputs are finite; a program needn't handle non-finite values. No bound on the sum of `gap_mask` on one device may be relied on, other than what follows from the above.
Results may differ from the reference program's by a relative error of at most 0.0003.
Values may be sent and summed in bfloat16 or wider, within the bound.
A program may use at most 128 MiB of HBM per device.

```python
import math
import jax
import jax.numpy as jnp
from jax import lax

SB = 8
SAMPLES = 2048
F = 1024
LAGS = 512
WBLK = 128
REACH = 2
STATIONS = 128
WINDOWS = 128
N_STA = 16


def draw_traces(key, part):
    source_key = jax.random.fold_in(key, 101)
    delay_key = jax.random.fold_in(key, 202)
    sign_key = jax.random.fold_in(key, 303)
    noise_key = jax.random.fold_in(key, 404)
    strength_key = jax.random.fold_in(key, 505)
    source = jnp.clip(jax.random.normal(source_key, (WINDOWS, SAMPLES), jnp.float32), -6.0, 6.0)
    delays = jax.random.randint(delay_key, (STATIONS,), 0, LAGS // 4).astype(jnp.int32)
    polarity = jax.random.randint(sign_key, (STATIONS,), 0, 2).astype(jnp.float32) * 2.0 - 1.0
    noise = jnp.clip(jax.random.normal(noise_key, (STATIONS, WINDOWS, SAMPLES), jnp.float32), -6.0, 6.0)
    strength = jnp.exp(jax.random.uniform(strength_key, (STATIONS,), jnp.float32, 0.0, math.log(3.0)))
    positions = (jnp.arange(SAMPLES, dtype=jnp.int32)[None, :] - delays[:, None]) % SAMPLES
    moved = jnp.take(source, positions, axis=1)
    coherent = jnp.transpose(moved, (1, 0, 2))
    return ((strength * polarity)[:, None, None] * coherent + noise).astype(jnp.float32)


def draw_pair_mask(key, part):
    choose_key = jax.random.fold_in(key, 606)
    kept = (jax.random.randint(choose_key, (STATIONS, 2 * REACH + 1, SB), 0, 5) < 4).astype(jnp.int32)
    station = jnp.arange(STATIONS, dtype=jnp.int32) % SB
    offset = jnp.arange(2 * REACH + 1, dtype=jnp.int32)
    partner = jnp.arange(SB, dtype=jnp.int32)
    itself = (station[:, None, None] == partner[None, None, :]) & (offset[None, :, None] == REACH)
    return jnp.where(itself, 0, kept).astype(jnp.int32)


def plant(array, own_key, smallest, high):
    extent = array.shape
    index_at = [jax.random.randint(jax.random.fold_in(own_key, axis), (), 0, extent[axis]) for axis in range(len(extent))]
    array = array.at[tuple(index_at)].set(smallest)
    longest = extent.index(max(extent))
    index_at[longest] = (index_at[longest] + 1) % extent[longest]
    return array.at[tuple(index_at)].set(high)


def setup_inputs(seed: int = 0) -> dict:
    seeds = jax.random.split(jax.random.key(seed), 4)
    return {
        "traces": draw_traces(jax.random.fold_in(seeds[3], 71), 0),
        "gap_mask": plant((jax.random.randint(seeds[1], (STATIONS, WINDOWS), 0, 4) < 3).astype(jnp.int32), jax.random.fold_in(seeds[1], 1), 0, 1),
        "pair_mask": draw_pair_mask(jax.random.fold_in(seeds[3], 71), 0),
    }


def transform_table():
    moments = jnp.arange(SAMPLES, dtype=jnp.int32)
    frequency = jnp.arange(F, dtype=jnp.int32)
    product = moments[:, None] * frequency[None, :] % SAMPLES
    angle = product.astype(jnp.float32) * (2.0 * math.pi / SAMPLES)
    return jnp.concatenate([jnp.cos(angle), -jnp.sin(angle)], axis=1)

def inverse_table():
    frequency = jnp.arange(F, dtype=jnp.int32)
    delays = jnp.arange(LAGS, dtype=jnp.int32) - LAGS // 2
    product = frequency[:, None] * delays[None, :] % SAMPLES
    angle = product.astype(jnp.float32) * (2.0 * math.pi / SAMPLES)
    cosine = jnp.cos(angle)
    sine = jnp.sin(angle)
    upper = jnp.concatenate([cosine, sine], axis=1)
    lower = jnp.concatenate([-sine, cosine], axis=1)
    return (jnp.concatenate([upper, lower], axis=0) * (1.0 / math.sqrt(F))).astype(jnp.bfloat16)

def whiten(traces):
    signs = jnp.sign(traces.astype(jnp.float32))
    flat = signs.reshape(-1, SAMPLES)
    spectra = jnp.dot(flat, transform_table(), precision=lax.Precision.HIGHEST, preferred_element_type=jnp.float32)
    real_part = spectra[:, :F]
    imag_part = spectra[:, F:]
    power = real_part * real_part + imag_part * imag_part
    bands = lax.optimization_barrier(jnp.mean(power.reshape(-1, F // WBLK, WBLK), axis=2))
    factor = 1.0 / jnp.sqrt(bands + 1e-05)
    factor = jnp.repeat(factor, WBLK, axis=1)
    white = jnp.concatenate([real_part * factor, imag_part * factor], axis=1).astype(jnp.bfloat16)
    return white.reshape(traces.shape[0], traces.shape[1], 2 * F)

def pair_terms(own_spectra, own_flags, far_spectra, far_flags, table):
    bin_count = own_spectra.shape[-1] // 2
    own_real = own_spectra[..., :bin_count].astype(jnp.float32)[:, None]
    own_imag = own_spectra[..., bin_count:].astype(jnp.float32)[:, None]
    far_real = far_spectra[..., :bin_count].astype(jnp.float32)[None]
    far_imag = far_spectra[..., bin_count:].astype(jnp.float32)[None]
    cross_real = own_real * far_real + own_imag * far_imag
    cross_imag = own_imag * far_real - own_real * far_imag
    cross = jnp.concatenate([cross_real, cross_imag], axis=-1).astype(jnp.bfloat16)
    lead = cross.shape[:3]
    analytic = jnp.dot(cross.reshape(-1, 2 * bin_count), table, preferred_element_type=jnp.float32)
    lag_count = table.shape[1] // 2
    analytic = analytic.reshape(lead + (2 * lag_count,))
    real_part = analytic[..., :lag_count]
    imag_part = analytic[..., lag_count:]
    magnitude = jnp.sqrt(real_part * real_part + imag_part * imag_part)
    divisor = jnp.maximum(magnitude, 0.5)
    weights = own_flags[:, None, :] * far_flags[None, :, :]
    linear = lax.optimization_barrier(jnp.sum(weights[..., None] * real_part, axis=2))
    phase_real = lax.optimization_barrier(jnp.sum(weights[..., None] * (real_part / divisor), axis=2))
    phase_imag = lax.optimization_barrier(jnp.sum(weights[..., None] * (imag_part / divisor), axis=2))
    counts = lax.optimization_barrier(jnp.sum(weights, axis=2))
    return (linear, phase_real, phase_imag, counts)

def reference(traces, gap_mask, pair_mask):
    white = whiten(traces)
    flags = gap_mask.astype(jnp.float32)
    table = inverse_table()
    blocks = white.reshape(N_STA, SB, white.shape[1], 2 * F)
    flag_blocks = flags.reshape(N_STA, SB, flags.shape[1])
    gathered = []
    for offset in range(2 * REACH + 1):
        moved = offset - REACH
        far_blocks = jnp.roll(blocks, -moved, axis=0)
        far_flags = jnp.roll(flag_blocks, -moved, axis=0)
        terms = lax.map(lambda items: pair_terms(items[0], items[1], items[2], items[3], table), (blocks, flag_blocks, far_blocks, far_flags))
        gathered.append(terms)
    linear = jnp.stack([item[0] for item in gathered], axis=2).reshape(N_STA * SB, 2 * REACH + 1, SB, LAGS)
    phase_real = jnp.stack([item[1] for item in gathered], axis=2).reshape(N_STA * SB, 2 * REACH + 1, SB, LAGS)
    phase_imag = jnp.stack([item[2] for item in gathered], axis=2).reshape(N_STA * SB, 2 * REACH + 1, SB, LAGS)
    counts = jnp.stack([item[3] for item in gathered], axis=2).reshape(N_STA * SB, 2 * REACH + 1, SB)
    divisor = jnp.maximum(counts, 1.0)[..., None]
    phase_real = phase_real / divisor
    phase_imag = phase_imag / divisor
    return linear / divisor * (phase_real * phase_real + phase_imag * phase_imag) * pair_mask.astype(jnp.float32)[..., None]
```

```python
import functools

import jax
import jax.numpy as jnp
import ml_dtypes
import numpy as np
from jax import lax
from jax.experimental import pallas as pl
from jax.experimental.pallas import tpu as pltpu
from jax.sharding import PartitionSpec as P

MESH = pl.DeviceIdType.MESH
SAMPLES = 2048
F = 1024
SB = 8
NW = 16
WIN = 8
ROOT = 0.7071067811865476
BF = jnp.bfloat16
F32 = jnp.float32

LANE = np.arange(128)
LANE_K = (LANE % 8) * 16 + LANE // 8


def class_frequency(r):
    return r + 8 * LANE_K


def forward_table():
    moment = np.arange(256)

    def trig(frequency):
        angle = (moment[:, None] * frequency[None, :] % SAMPLES) * (2.0 * np.pi / SAMPLES)
        return np.cos(angle), np.sin(angle)

    columns = []
    for r in (1, 3, 2):
        ca, sa = trig(class_frequency(r))
        cb, sb = trig(SAMPLES - class_frequency(8 - r))
        columns += [ca, cb, sa, sb]
    for r in (0, 4):
        columns += list(trig(class_frequency(r)))
    rest = np.concatenate(columns, axis=1).astype(np.float32)
    parts = []
    for _ in range(3):
        part = rest.astype(ml_dtypes.bfloat16)
        parts.append(part)
        rest = rest - part.astype(np.float32)
    return np.concatenate(parts, axis=0)


def inverse_table():
    frequency = np.concatenate([class_frequency(r) for r in range(8)])
    lag = np.arange(256)
    sine_lag = np.where(lag == 0, 256, lag)

    def angle(t):
        return (frequency[:, None] * t[None, :] % SAMPLES) * (2.0 * np.pi / SAMPLES)

    both = np.concatenate([np.cos(angle(lag)), np.sin(angle(sine_lag))], axis=1)
    return (both.astype(np.float32) * np.float32(1.0 / 32.0)).astype(ml_dtypes.bfloat16)


LAST_ONE = float(np.float32(1.0 / 32.0))
LAST_ROOT = float(np.float32(np.float32(ROOT) / 32.0).astype(ml_dtypes.bfloat16))


def lanes(shape):
    return lax.broadcasted_iota(jnp.int32, shape, len(shape) - 1)


def spectrum_parts(res, rows):
    r1, r3, r2, r0, r4 = res

    def get(ref, block, lo, hi):
        return ref[pl.ds(block * 128 + rows, 16), lo:hi]

    real, imag = [None] * 8, [None] * 8

    def both(r, yrc, yrs, yic, yis):
        xr, xi = yrc + yis, yic - yrs
        real[r], imag[r] = xr[:, :128], xi[:, :128]
        real[8 - r], imag[8 - r] = xr[:, 128:], -xi[:, 128:]

    both(
        1,
        get(r1, 0, 0, 256) + ROOT * get(r1, 1, 0, 256),
        get(r1, 0, 256, 512) + ROOT * get(r1, 1, 256, 512),
        -(get(r1, 2, 0, 256) + ROOT * get(r1, 3, 0, 256)),
        -(get(r1, 2, 256, 512) + ROOT * get(r1, 3, 256, 512)),
    )
    both(
        3,
        get(r3, 0, 0, 256) - ROOT * get(r3, 1, 0, 256),
        get(r3, 0, 256, 512) - ROOT * get(r3, 1, 256, 512),
        get(r3, 2, 0, 256) - ROOT * get(r3, 3, 0, 256),
        get(r3, 2, 256, 512) - ROOT * get(r3, 3, 256, 512),
    )
    both(2, get(r2, 0, 0, 256), get(r2, 0, 256, 512), -get(r2, 1, 0, 256), -get(r2, 1, 256, 512))
    for r, ref in ((0, r0), (4, r4)):
        real[r], imag[r] = get(ref, 0, 0, 128), -get(ref, 0, 128, 256)
    return real, imag


def kernel(
    n_sta,
    traces_ref,
    gap_ref,
    ftab_ref,
    itab_ref,
    out_ref,
    tr,
    ftab,
    itab,
    folded,
    r1,
    r3,
    r2,
    r0,
    r4,
    white,
    own,
    far,
    lhs,
    res,
    flags,
    flags_in,
    all_flags,
    counts,
    counts_in,
    packed,
    packed_in,
    last,
    last_in,
    stack,
    stack2,
    mirror,
    mirror2,
    load_sem,
    flag_send,
    flag_recv,
    up_send,
    two_send,
    pass_send,
    white_recv,
    count_send,
    count_recv,
    red_send,
    red_recv,
    last_send,
    last_recv,
    mir_send,
    mir_recv,
):
    sta = lax.axis_index("sta")
    win = lax.axis_index("win")
    odd = lax.rem(sta, 2) == 1

    def at_sta(d):
        return lax.rem(sta + d + n_sta, n_sta)

    def at_win(o):
        return lax.rem(win + o, WIN)

    loads = [
        pltpu.make_async_copy(traces_ref, tr, load_sem.at[0]),
        pltpu.make_async_copy(ftab_ref, ftab, load_sem.at[1]),
        pltpu.make_async_copy(itab_ref, itab, load_sem.at[2]),
    ]
    for load in loads:
        load.start()

    barrier = pltpu.get_barrier_semaphore()
    flip, turn = 7 - win, lax.rem(8 - win, WIN)
    friends = [(at_sta(d), win) for d in (-2, -1, 1, 2)]
    friends += [(sta, at_win(o)) for o in range(1, WIN)]
    friends += [(at_sta(d), w) for d in (-2, -1, 1, 2) for w in (flip, turn)]
    for friend in friends:
        pl.semaphore_signal(barrier, inc=1, device_id=friend, device_id_type=MESH)

    flags[...] = jnp.zeros_like(flags)
    flags[:, 0:NW] = gap_ref[...].astype(F32)
    all_flags[...] = jnp.zeros_like(all_flags)
    all_flags[0:8, :] = flags[...]
    last[...] = jnp.zeros_like(last)

    loads[0].wait()

    def fold(s, carry):
        row = pl.multiple_of(s * 16, 16)

        def sign(a):
            v = tr[pl.ds(row, 16), a * 256 : (a + 1) * 256]
            return jnp.where(v > 0, 1.0, 0.0) - jnp.where(v < 0, 1.0, 0.0)

        x = [sign(a) for a in range(8)]
        s04, s15, s26, s37 = [x[a] + x[a + 4] for a in range(4)]
        d04, d15, d26, d37 = [x[a] - x[a + 4] for a in range(4)]
        rows = [d04, d15 - d37, d26, d15 + d37, s04 - s26, s15 - s37]
        even, other = s04 + s26, s15 + s37
        rows += [even + other, even - other]
        for n, v in enumerate(rows):
            folded[pl.ds(pl.multiple_of(n * 128 + row, 16), 16), :] = v.astype(BF)
        return carry

    lax.fori_loop(0, 8, fold, 0)
    loads[1].wait()

    def transform(dst, first, count, column, width):
        y = folded[first * 128 : (first + count) * 128, :]
        y = jnp.concatenate([y, y, y], axis=1)
        dst[...] = jnp.dot(y, ftab[:, column : column + width], preferred_element_type=F32)

    transform(r1, 0, 4, 0, 512)
    transform(r3, 0, 4, 512, 512)
    transform(r2, 4, 2, 1024, 512)
    transform(r0, 6, 1, 1536, 256)
    transform(r4, 7, 1, 1792, 256)

    pl.semaphore_wait(barrier, len(friends))

    def flag_copy(d):
        return pltpu.make_async_remote_copy(
            flags, flags_in.at[d - 1], flag_send.at[d - 1], flag_recv.at[d - 1],
            device_id=(at_sta(-d), win), device_id_type=MESH,
        )

    for d in (1, 2):
        flag_copy(d).start()

    def up_copy(j):
        return pltpu.make_async_remote_copy(
            white.at[0, j], white.at[1, j], up_send.at[j], white_recv.at[0, j],
            device_id=(at_sta(-1), win), device_id_type=MESH,
        )

    def two_copy(j):
        return pltpu.make_async_remote_copy(
            white.at[0, j], white.at[2, j], two_send.at[j], white_recv.at[1, j],
            device_id=(at_sta(-2), win), device_id_type=MESH,
        )

    def pass_copy(j):
        return pltpu.make_async_remote_copy(
            white.at[1, j], white.at[2, j], pass_send.at[j], white_recv.at[1, j],
            device_id=(at_sta(-1), win), device_id_type=MESH,
        )

    def whiten(s, carry):
        row = pl.multiple_of(s * 16, 16)
        real, imag = spectrum_parts((r1, r3, r2, r0, r4), row)
        power = real[0] * real[0] + imag[0] * imag[0]
        for r in range(1, 8):
            power = power + (real[r] * real[r] + imag[r] * imag[r])
        for shift in (8, 16, 32, 64):
            power = power + pltpu.roll(power, shift, 1)
        band = power * (1.0 / 128.0)
        flag = jnp.broadcast_to(flags[pl.ds(s, 1), :], (16, 128))
        eye = lanes((16, 128)) == lax.broadcasted_iota(jnp.int32, (16, 128), 0)
        flag = jnp.sum(jnp.where(eye, flag, 0.0), axis=1, keepdims=True)
        factor = 1.0 / jnp.sqrt(band + 1e-05) * flag
        for r in range(8):
            for half, v in ((0, real[r]), (1024, imag[r])):
                v = (v * factor).astype(BF)
                c = half + r * 128
                white[0, pl.ds(s, 1), :, c : c + 128] = v[None]
                own[c // 128, pl.ds(s, 16, stride=8), :] = v.astype(F32)
        up_copy(s).start()

        @pl.when(odd)
        def _():
            two_copy(s).start()

        return carry

    lax.fori_loop(0, 8, whiten, 0)
    loads[2].wait()

    lane = lanes((8, 128))
    first_lane = lane == 0
    low = lane < 64

    def unit(k, j):
        far[...] = white[pl.ds(k, 1), pl.ds(j, 1)][0, 0].astype(F32)
        ends = []
        for wp in range(8):
            rows = slice(16 * wp, 16 * wp + 16)
            t = [None] * 4
            sums = [[0.0, 0.0], [0.0, 0.0]]
            for r in range(8):
                c = slice(128 * r, 128 * r + 128)
                ci = slice(1024 + 128 * r, 1152 + 128 * r)
                ar, ai = own[r, rows, :], own[8 + r, rows, :]

                def spread(cols):
                    return jnp.concatenate(
                        [jnp.broadcast_to(far[2 * wp + h : 2 * wp + h + 1, cols], (8, 128)) for h in (0, 1)], axis=0
                    )

                br, bi = spread(c), spread(ci)
                for which, v in ((0, ar * br + ai * bi), (1, ai * br - ar * bi)):
                    lhs[slice(which * 128 + 16 * wp, which * 128 + 16 * wp + 16), c] = v.astype(BF)
                    if r in (0, 4):
                        sums[which][0] = sums[which][0] + (v if r == 0 else -v)
                    elif r in (1, 3, 5, 7):
                        sums[which][1] = sums[which][1] + (v if r in (1, 7) else -v)
            ends.append([
                jnp.sum(s0 * LAST_ONE + s1 * LAST_ROOT, axis=1, keepdims=True) for s0, s1 in sums
            ])
        res[...] = jnp.dot(lhs[...], itab[...], preferred_element_type=F32)
        zero = jnp.zeros((8, 128), F32)
        total = [[zero] * 3 for _ in range(5)]

        def add(n, re, im):
            scale = lax.rsqrt(jnp.maximum(re * re + im * im, 0.25))
            total[n][0] = total[n][0] + re
            total[n][1] = total[n][1] + re * scale
            total[n][2] = total[n][2] + im * scale

        for w in range(NW):
            re_rows, im_rows = slice(8 * w, 8 * w + 8), slice(128 + 8 * w, 136 + 8 * w)
            for tile in range(2):
                cos, sin = slice(128 * tile, 128 * tile + 128), slice(256 + 128 * tile, 384 + 128 * tile)
                a, c = res[re_rows, cos], res[re_rows, sin]
                d, b = res[im_rows, cos], res[im_rows, sin]
                if tile == 0:
                    h = 8 * (w % 2)
                    end_re, end_im = [v[h : h + 8] for v in ends[w // 2]]
                    add(0, a - jnp.where(first_lane, 0.0, b), d + jnp.where(first_lane, 0.0, c))
                    a, d = jnp.where(first_lane, end_re, a), jnp.where(first_lane, end_im, d)
                    add(4, a - b, d + c)
                else:
                    add(1, a - b, d + c)
                add(2 + tile, a + b, d - c)
        out = []
        for q in range(3):
            neg = pltpu.roll(jnp.concatenate([total[2][q], total[3][q]], axis=1), 255, 1)
            out.append([total[0][q], total[1][q], neg[:, :128], neg[:, 128:], total[4][q]])
        return out

    def which_pair(d):
        e = jnp.maximum(d - 4, 0)
        early = d < 4
        k = jnp.where(early, 0, 1 + lax.rem(e, 2))
        jj = jnp.where(early, d, e // 2)
        return k, jj

    def red_copy(d, o):
        return pltpu.make_async_remote_copy(
            packed.at[d, at_win(o)], packed_in.at[d, o - 1], red_send.at[d, o - 1], red_recv.at[d, o - 1],
            device_id=(sta, at_win(o)), device_id_type=MESH,
        )

    def count_copy(o):
        return pltpu.make_async_remote_copy(
            counts, counts_in.at[o - 1], count_send.at[o - 1], count_recv.at[o - 1],
            device_id=(sta, at_win(o)), device_id_type=MESH,
        )

    def step(d, carry):
        k, jj = which_pair(d)

        @pl.when(d == 4)
        def _():
            for m in (1, 2):
                flag_copy(m).wait_recv()
                all_flags[8 * m : 8 * m + 8, :] = flags_in[m - 1]
            counts[...] = lax.dot_general(
                flags[...].astype(BF), all_flags[...].astype(BF), (((1,), (1,)), ((), ())), preferred_element_type=F32
            )
            for o in range(1, WIN):
                count_copy(o).start()

        @pl.when(k == 1)
        def _():
            for h in (0, 1):
                up_copy(2 * jj + h).wait_recv()

                @pl.when(odd)
                def _():
                    pass_copy(2 * jj + h).start()

        @pl.when(k == 2)
        def _():
            for h in (0, 1):
                two_copy(2 * jj + h).wait_recv()

        one = unit(k, 2 * jj)
        two = unit(k, 2 * jj + 1)
        for q in range(3):
            rows = slice(8 * q, 8 * q + 8)
            for n in range(4):
                x, y = one[q][n], two[q][n]
                left = jnp.where(low, x, pltpu.roll(y, 64, 1))
                right = jnp.where(low, pltpu.roll(x, 64, 1), y)
                if n < 2:
                    places = (4 + 2 * n, 5 + 2 * n)
                else:
                    places = (3 - 2 * (n - 2), 2 - 2 * (n - 2))
                for place, v in zip(places, (left, right)):
                    packed[pl.ds(d, 1), place, rows, :] = v[None]
            code = k * 8 + 2 * jj
            e = last[rows, :]
            e = jnp.where(lane == code, one[q][4][:, 0:1], e)
            last[rows, :] = jnp.where(lane == code + 1, two[q][4][:, 0:1], e)
        for o in range(1, WIN):
            red_copy(d, o).start()
        return carry

    lax.fori_loop(0, 12, step, 0)

    def last_copy(slot):
        return pltpu.make_async_remote_copy(
            last, last_in.at[slot], last_send.at[0], last_recv.at[slot],
            device_id=(sta, 0), device_id_type=MESH,
        )

    @pl.when(win != 0)
    def _():
        last_copy(7 - win).start()

    total_count = counts[...]
    for o in range(1, WIN):
        count_copy(o).wait_recv()
        total_count = total_count + counts_in[o - 1]

    def weighted(lin, pr, pi, count):
        inverse = 1.0 / jnp.maximum(count, 1.0)
        pr, pi = pr * inverse, pi * inverse
        return lin * inverse * (pr * pr + pi * pi)

    def mir_copy(n, which, k):
        src, dst, to = ((stack, mirror, flip), (stack2, mirror2, turn))[which]
        return pltpu.make_async_remote_copy(
            src.at[n], dst.at[n - 4], mir_send.at[n - 4, which], mir_recv.at[n - 4, which],
            device_id=(at_sta(k), to), device_id_type=MESH,
        )

    def pick(v, at):
        return jnp.sum(jnp.where(lane == at, v, 0.0), axis=1, keepdims=True)

    def finish(d):
        k, jj = (0, d) if d < 4 else (1 + (d - 4) % 2, (d - 4) // 2)
        v = packed[d, pl.ds(win, 1)][0]
        for o in range(1, WIN):
            red_copy(d, o).wait_recv()
            v = v + packed_in[d, o - 1]
        code = k * 8 + 2 * jj
        count = jnp.where(low, total_count[:, code : code + 1], total_count[:, code + 1 : code + 2])
        stack[d] = weighted(v[0:8], v[8:16], v[16:24], count)
        if k:
            mir_copy(d, 0, k).start()

            @pl.when(win != 0)
            def _():
                stack2[d] = stack[d]
                mir_copy(d, 1, k).start()

    for d in range(12):
        finish(d)

    @pl.when(win == 0)
    def _():
        e = last[...]
        for slot in range(7):
            last_copy(slot).wait_recv()
            e = e + last_in[slot]
        end = weighted(e[0:8], e[8:16], e[16:24], total_count)
        for d in range(4, 12):
            k, jj = 1 + (d - 4) % 2, (d - 4) // 2
            code = k * 8 + 2 * jj
            v = jnp.where(lane == 63, end[:, code : code + 1], stack[d])
            stack2[d] = jnp.where(lane == 127, end[:, code + 1 : code + 2], v)
            mir_copy(d, 1, k).start()

    row_id = lax.broadcasted_iota(jnp.int32, (128, 128), 0)
    col_id = lanes((128, 128))
    half, place = col_id // 64, lax.rem(col_id, 64)
    lower = win < 4
    take = half * 64 + jnp.where(lower, 63 - place, place)
    direct = jnp.where(row_id == take, 1.0, 0.0)
    take = half * 64 + jnp.where(lower, 64 - place, place - 1)
    mirrored = jnp.where((row_id == take) & (place != 0), 1.0, 0.0)
    take = half * 64 + jnp.where(turn < 4, 63, 0)
    ending = jnp.where((row_id == take) & (place == 0), 1.0, 0.0)

    def ordered(v, table):
        return jnp.dot(v, table, precision=lax.Precision.HIGHEST, preferred_element_type=F32)

    v = ordered(stack[...].reshape(96, 128), direct)
    for d in range(12):
        k, jj = (0, d) if d < 4 else (1 + (d - 4) % 2, (d - 4) // 2)
        t = v[8 * d : 8 * d + 8]
        at = (k + 2) * 8 + 2 * jj
        out_ref[pl.ds(at, 8, stride=40), :] = t
        out_ref[pl.ds(at + 1, 8, stride=40), :] = pltpu.roll(t, 64, 1)

    for d in range(4, 12):
        k = 1 + (d - 4) % 2
        for which in (0, 1):
            mir_copy(d, which, k).wait_recv()
    v = ordered(mirror[...].reshape(64, 128), mirrored) + ordered(mirror2[...].reshape(64, 128), ending)
    for n in range(8):
        k, jj = 1 + n % 2, n // 2
        t = v[8 * n : 8 * n + 8]
        at = 2 * jj * 40 + (2 - k) * 8
        out_ref[at : at + 8, :] = t
        out_ref[at + 40 : at + 48, :] = pltpu.roll(t, 64, 1)

    for d in (1, 2):
        flag_copy(d).wait_send()
    for j in range(8):
        up_copy(j).wait_send()

    @pl.when(odd)
    def _():
        for j in range(8):
            two_copy(j).wait_send()
            pass_copy(j).wait_send()

    for o in range(1, WIN):
        count_copy(o).wait_send()

    def drain(d, carry):
        for o in range(1, WIN):
            red_copy(d, o).wait_send()
        return carry

    lax.fori_loop(0, 12, drain, 0)

    @pl.when(win != 0)
    def _():
        last_copy(7 - win).wait_send()

    for d in range(4, 12):
        for which in (0, 1):
            mir_copy(d, which, 1 + (d - 4) % 2).wait_send()


def local(n_sta, traces, gap_mask, pair_mask):
    vmem, dma = pltpu.VMEM, pltpu.SemaphoreType.DMA
    anywhere = pl.BlockSpec(memory_space=pl.ANY)
    inside = pl.BlockSpec(memory_space=pltpu.VMEM)
    stacked = pl.pallas_call(
        functools.partial(kernel, n_sta),
        out_shape=jax.ShapeDtypeStruct((320, 128), F32),
        in_specs=[anywhere, inside, anywhere, anywhere],
        out_specs=inside,
        scratch_shapes=[
            vmem((128, 2048), F32),
            vmem((768, 2048), BF),
            vmem((1024, 512), BF),
            vmem((1024, 256), BF),
            vmem((512, 512), F32),
            vmem((512, 512), F32),
            vmem((256, 512), F32),
            vmem((128, 256), F32),
            vmem((128, 256), F32),
            vmem((3, 8, 16, 2048), BF),
            vmem((16, 128, 128), F32),
            vmem((16, 2048), F32),
            vmem((256, 1024), BF),
            vmem((256, 512), F32),
            vmem((8, 128), F32),
            vmem((2, 8, 128), F32),
            vmem((128, 128), F32),
            vmem((8, 128), F32),
            vmem((7, 8, 128), F32),
            vmem((12, 8, 24, 128), F32),
            vmem((12, 7, 24, 128), F32),
            vmem((24, 128), F32),
            vmem((7, 24, 128), F32),
            vmem((12, 8, 128), F32),
            vmem((12, 8, 128), F32),
            vmem((8, 8, 128), F32),
            vmem((8, 8, 128), F32),
            dma((3,)),
            dma((2,)),
            dma((2,)),
            dma((8,)),
            dma((8,)),
            dma((8,)),
            dma((2, 8)),
            dma((7,)),
            dma((7,)),
            dma((12, 7)),
            dma((12, 7)),
            dma((1,)),
            dma((7,)),
            dma((8, 2)),
            dma((8, 2)),
        ],
        compiler_params=pltpu.CompilerParams(
            collective_id=0, has_side_effects=True, vmem_limit_bytes=48 * 1024 * 1024
        ),
    )(traces.reshape(128, SAMPLES), gap_mask, jnp.asarray(forward_table()), jnp.asarray(inverse_table()))
    return stacked.reshape(8, 5, 8, 128)[..., :64] * pair_mask.astype(F32)[..., None]


def solution(mesh):
    return jax.shard_map(
        functools.partial(local, mesh.shape["sta"]),
        mesh=mesh,
        in_specs=(P("sta", "win", None), P("sta", "win"), P("sta", None, None)),
        out_specs=P("sta", None, None, "win"),
        check_vma=False,
    )
```

```python
import functools

import jax
import jax.numpy as jnp
import ml_dtypes
import numpy as np
from jax import lax
from jax.experimental import pallas as pl
from jax.experimental.pallas import tpu as pltpu
from jax.sharding import PartitionSpec as P

MESH = pl.DeviceIdType.MESH
SAMPLES = 2048
F = 1024
SB = 8
NW = 16
WIN = 8
ROOT = 0.7071067811865476
BF = jnp.bfloat16
F32 = jnp.float32

LANE = np.arange(128)
LANE_K = (LANE % 8) * 16 + LANE // 8


ORDER = (0, 4, 1, 5, 3, 7, 2, 6)


def class_frequency(r):
    return r + 8 * LANE_K


def forward_table():
    moment = np.arange(256)

    def trig(frequency):
        angle = (moment[:, None] * frequency[None, :] % SAMPLES) * (2.0 * np.pi / SAMPLES)
        return np.cos(angle), np.sin(angle)

    columns = []
    for r in (1, 3, 2):
        ca, sa = trig(class_frequency(r))
        cb, sb = trig(SAMPLES - class_frequency(8 - r))
        columns += [ca, cb, sa, sb]
    for r in (0, 4):
        columns += list(trig(class_frequency(r)))
    rest = np.concatenate(columns, axis=1).astype(np.float32)
    parts = []
    for _ in range(3):
        part = rest.astype(ml_dtypes.bfloat16)
        parts.append(part)
        rest = rest - part.astype(np.float32)
    return np.concatenate(parts, axis=0)


def inverse_table():
    frequency = np.concatenate([class_frequency(r) for r in ORDER])
    lag = np.arange(256)
    sine_lag = np.where(lag == 0, 256, lag)

    def angle(t):
        return (frequency[:, None] * t[None, :] % SAMPLES) * (2.0 * np.pi / SAMPLES)

    both = np.concatenate([np.cos(angle(lag)), np.sin(angle(sine_lag))], axis=1)
    return (both.astype(np.float32) * np.float32(1.0 / 32.0)).astype(ml_dtypes.bfloat16)


LIN_CODE = 1430.0
PHASE_CODE = 2047.0
END_ONE = 1.0 / 32.0
END_RATIO = float(np.float32(ROOT).astype(ml_dtypes.bfloat16))


def lanes(shape):
    return lax.broadcasted_iota(jnp.int32, shape, len(shape) - 1)


def spectrum_parts(res, rows):
    r1, r3, r2, r0, r4 = res

    def get(ref, block, lo, hi):
        return ref[pl.ds(block * 128 + rows, 16), lo:hi]

    real, imag = [None] * 8, [None] * 8

    def both(r, yrc, yrs, yic, yis):
        xr, xi = yrc + yis, yic - yrs
        real[r], imag[r] = xr[:, :128], xi[:, :128]
        real[8 - r], imag[8 - r] = xr[:, 128:], -xi[:, 128:]

    both(
        1,
        get(r1, 0, 0, 256) + ROOT * get(r1, 1, 0, 256),
        get(r1, 0, 256, 512) + ROOT * get(r1, 1, 256, 512),
        -(get(r1, 2, 0, 256) + ROOT * get(r1, 3, 0, 256)),
        -(get(r1, 2, 256, 512) + ROOT * get(r1, 3, 256, 512)),
    )
    both(
        3,
        get(r3, 0, 0, 256) - ROOT * get(r3, 1, 0, 256),
        get(r3, 0, 256, 512) - ROOT * get(r3, 1, 256, 512),
        get(r3, 2, 0, 256) - ROOT * get(r3, 3, 0, 256),
        get(r3, 2, 256, 512) - ROOT * get(r3, 3, 256, 512),
    )
    both(2, get(r2, 0, 0, 256), get(r2, 0, 256, 512), -get(r2, 1, 0, 256), -get(r2, 1, 256, 512))
    for r, ref in ((0, r0), (4, r4)):
        real[r], imag[r] = get(ref, 0, 0, 128), -get(ref, 0, 128, 256)
    return real, imag


def kernel(
    n_sta,
    traces_ref,
    gap_ref,
    keep_ref,
    ftab_ref,
    itab_ref,
    out_ref,
    gap,
    keep_in,
    tr,
    ftab,
    itab,
    folded,
    r1,
    r3,
    r2,
    r0,
    r4,
    white,
    own,
    far,
    lhs,
    res,
    edge,
    flags,
    flags_in,
    keep_all,
    all_flags,
    counts,
    counts_in,
    count_sum,
    sums,
    ends_sum,
    packed,
    packed_in,
    kept,
    half,
    half_in,
    stack,
    stack2,
    mirror,
    mirror2,
    ready,
    load_sem,
    flag_send,
    flag_recv,
    up_send,
    two_send,
    pass_send,
    white_recv,
    count_send,
    count_recv,
    red_send,
    red_recv,
    half_send,
    half_recv,
    mir_send,
    mir_recv,
):
    sta = lax.axis_index("sta")
    win = lax.axis_index("win")
    odd = lax.rem(sta, 2) == 1

    def at_sta(d):
        return lax.rem(sta + d + n_sta, n_sta)

    def at_win(o):
        return lax.rem(win + o, WIN)

    loads = [
        pltpu.make_async_copy(traces_ref, tr, load_sem.at[0]),
        pltpu.make_async_copy(ftab_ref, ftab, load_sem.at[1]),
        pltpu.make_async_copy(itab_ref, itab, load_sem.at[2]),
        pltpu.make_async_copy(gap_ref, gap, load_sem.at[3]),
        pltpu.make_async_copy(keep_ref, keep_in, load_sem.at[4]),
    ]
    for load in loads:
        load.start()

    barrier = pltpu.get_barrier_semaphore()
    flip, turn = 7 - win, lax.rem(8 - win, WIN)
    high, level = win // 4, lax.rem(win, 4)
    across = (sta, lax.rem(win + 4, WIN))
    near = [(at_sta(d), win) for d in (-2, -1, 1, 2)]
    near += [(sta, high * 4 + lax.rem(level + d, 4)) for d in (1, 3)]
    near += [across]
    for friend in near:
        pl.semaphore_signal(barrier, inc=1, device_id=friend, device_id_type=MESH)

    def tell(t):
        for friend in near:
            pl.semaphore_signal(ready.at[t], inc=1, device_id=friend, device_id_type=MESH)

    def heard(t):
        pl.semaphore_wait(ready.at[t], len(near))

    flags[...] = jnp.zeros_like(flags)
    all_flags[...] = jnp.zeros_like(all_flags)
    ends_sum[...] = jnp.zeros_like(ends_sum)
    loads[0].wait()
    loads[3].wait()
    flags[:, 0:NW] = gap[...].astype(F32)
    all_flags[0:8, :] = flags[...]

    def fold(s, carry):
        row = pl.multiple_of(s * 16, 16)

        def sign(a):
            v = tr[pl.ds(row, 16), a * 256 : (a + 1) * 256]
            return jnp.where(v > 0, 1.0, 0.0) - jnp.where(v < 0, 1.0, 0.0)

        x = [sign(a) for a in range(8)]
        s04, s15, s26, s37 = [x[a] + x[a + 4] for a in range(4)]
        d04, d15, d26, d37 = [x[a] - x[a + 4] for a in range(4)]
        rows = [d04, d15 - d37, d26, d15 + d37, s04 - s26, s15 - s37]
        even, other = s04 + s26, s15 + s37
        rows += [even + other, even - other]
        for n, v in enumerate(rows):
            folded[pl.ds(pl.multiple_of(n * 128 + row, 16), 16), :] = v.astype(BF)
        return carry

    lax.fori_loop(0, 8, fold, 0)
    loads[1].wait()

    def transform(dst, first, count, column, width):
        y = folded[first * 128 : (first + count) * 128, :]
        y = jnp.concatenate([y, y, y], axis=1)
        dst[...] = jnp.dot(y, ftab[:, column : column + width], preferred_element_type=F32)

    transform(r1, 0, 4, 0, 512)
    transform(r3, 0, 4, 512, 512)
    transform(r2, 4, 2, 1024, 512)
    transform(r0, 6, 1, 1536, 256)
    transform(r4, 7, 1, 1792, 256)

    pl.semaphore_wait(barrier, len(near))
    tell(0)

    def flag_copy(d):
        return pltpu.make_async_remote_copy(
            flags, flags_in.at[d - 1], flag_send.at[d - 1], flag_recv.at[d - 1],
            device_id=(at_sta(-d), win), device_id_type=MESH,
        )

    for d in (1, 2):
        flag_copy(d).start()

    def up_copy(j):
        return pltpu.make_async_remote_copy(
            white.at[0, j], white.at[1, j], up_send.at[j], white_recv.at[0, j],
            device_id=(at_sta(-1), win), device_id_type=MESH,
        )

    def two_copy(j):
        return pltpu.make_async_remote_copy(
            white.at[0, j], white.at[2, j], two_send.at[j], white_recv.at[1, j],
            device_id=(at_sta(-2), win), device_id_type=MESH,
        )

    def pass_copy(j):
        return pltpu.make_async_remote_copy(
            white.at[1, j], white.at[2, j], pass_send.at[j], white_recv.at[1, j],
            device_id=(at_sta(-1), win), device_id_type=MESH,
        )

    def whiten(s, carry):
        row = pl.multiple_of(s * 16, 16)
        real, imag = spectrum_parts((r1, r3, r2, r0, r4), row)
        power = real[0] * real[0] + imag[0] * imag[0]
        for r in range(1, 8):
            power = power + (real[r] * real[r] + imag[r] * imag[r])
        for shift in (8, 16, 32, 64):
            power = power + pltpu.roll(power, shift, 1)
        band = power * (1.0 / 128.0)
        flag = jnp.broadcast_to(flags[pl.ds(s, 1), :], (16, 128))
        eye = lanes((16, 128)) == lax.broadcasted_iota(jnp.int32, (16, 128), 0)
        flag = jnp.sum(jnp.where(eye, flag, 0.0), axis=1, keepdims=True)
        factor = 1.0 / jnp.sqrt(band + 1e-05) * flag
        for r in range(8):
            for half, v in ((0, real[r]), (1024, imag[r])):
                v = (v * factor).astype(BF)
                c = half + r * 128
                white[0, pl.ds(s, 1), :, c : c + 128] = v[None]
                own[c // 128, pl.ds(s, 16, stride=8), :] = v.astype(F32)
        up_copy(s).start()

        @pl.when(odd)
        def _():
            two_copy(s).start()

        return carry

    lax.fori_loop(0, 8, whiten, 0)
    loads[2].wait()
    heard(0)
    tell(1)

    lane = lanes((8, 128))
    first_lane = lane == 0
    low = lane < 64

    def cross(k, jj):
        for h in (0, 1):
            far[h] = white[pl.ds(k, 1), pl.ds(2 * jj + h, 1)][0, 0].astype(F32)
        for m in range(4):
            for wp in range(8):
                rows = slice(16 * wp, 16 * wp + 16)
                ends = [None] * 4
                for p in (2 * m, 2 * m + 1):
                    r = ORDER[p]
                    ar, ai = own[r, rows, :], own[8 + r, rows, :]
                    for h in (0, 1):

                        def spread(r):
                            c = slice(128 * r, 128 * r + 128)
                            return jnp.concatenate(
                                [jnp.broadcast_to(far[h, 2 * wp + g : 2 * wp + g + 1, c], (8, 128)) for g in (0, 1)],
                                axis=0,
                            )

                        br, bi = spread(r), spread(8 + r)
                        for which, v in ((0, ar * br + ai * bi), (1, ai * br - ar * bi)):
                            at = h * 256 + which * 128 + 16 * wp
                            lhs[at : at + 16, 128 * p : 128 * p + 128] = v.astype(BF)
                            n = 2 * h + which
                            if m < 3:
                                plus = r in (0, 1, 7)
                                ends[n] = v if ends[n] is None else (ends[n] - v if not plus else v - ends[n])
                for n in range(4):
                    if m == 0:
                        edge[n, rows, :] = ends[n]
                    elif m == 1:
                        edge[n, rows, :] = edge[n, rows, :] + END_RATIO * ends[n]
                    elif m == 2:
                        v = edge[n, rows, :] + END_RATIO * ends[n]
                        v = jnp.sum(v * END_ONE, axis=1, keepdims=True)
                        edge[n, rows, :] = jnp.broadcast_to(v, (16, 128))

    def product():
        res[...] = jnp.dot(lhs[...], itab[...], preferred_element_type=F32)

    def collect(h):
        zero = jnp.zeros((8, 128), F32)
        total = [[zero] * 3 for _ in range(4)]
        end_re, end_im = zero, zero

        def parts(re, im):
            scale = lax.rsqrt(jnp.maximum(re * re + im * im, 0.25))
            return re, re * scale, im * scale

        def add(n, re, im):
            total[n] = [t + v for t, v in zip(total[n], parts(re, im))]

        for w in range(NW):
            wr = slice(8 * w, 8 * w + 8)
            re_rows = slice(256 * h + 8 * w, 256 * h + 8 * w + 8)
            im_rows = slice(256 * h + 128 + 8 * w, 256 * h + 136 + 8 * w)
            for tile in range(2):
                cos, sin = slice(128 * tile, 128 * tile + 128), slice(256 + 128 * tile, 384 + 128 * tile)
                a, c = res[re_rows, cos], res[re_rows, sin]
                d, b = res[im_rows, cos], res[im_rows, sin]
                if tile == 0:
                    edge_re, edge_im = edge[2 * h, wr, :], edge[2 * h + 1, wr, :]
                    add(0, a - jnp.where(first_lane, 0.0, b), d + jnp.where(first_lane, 0.0, c))
                    a, d = jnp.where(first_lane, edge_re, a), jnp.where(first_lane, edge_im, d)
                    x, y = a - b, d + c
                    if w:
                        x, y = pltpu.roll(x, w, 1), pltpu.roll(y, w, 1)
                    end_re, end_im = jnp.where(lane == w, x, end_re), jnp.where(lane == w, y, end_im)
                else:
                    add(1, a - b, d + c)
                add(2 + tile, a + b, d - c)
        end = [jnp.sum(v, axis=1, keepdims=True) for v in parts(end_re, end_im)]
        out = []
        for q in range(3):
            neg = pltpu.roll(jnp.concatenate([total[2][q], total[3][q]], axis=1), 255, 1)
            out.append([total[0][q], total[1][q], neg[:, :128], neg[:, 128:], end[q]])
        return out

    def post(g):
        one, two = collect(0), collect(1)
        for q in range(3):
            rows = slice(16 * q + 8 * g, 16 * q + 8 * g + 8)
            for n in range(4):
                x, y = one[q][n], two[q][n]
                left = jnp.where(low, x, pltpu.roll(y, 64, 1))
                right = jnp.where(low, pltpu.roll(x, 64, 1), y)
                if n < 2:
                    places = (4 + 2 * n, 5 + 2 * n)
                else:
                    places = (3 - 2 * (n - 2), 2 - 2 * (n - 2))
                for place, v in zip(places, (left, right)):
                    sums[place, rows, :] = v
            e = jnp.where(lane == 4 * q + 2 * g, one[q][3 + 1], ends_sum[...])
            ends_sum[...] = jnp.where(lane == 4 * q + 2 * g + 1, two[q][4], e)

    def to_code(v, root):
        if root is not None:
            r = jnp.sqrt(jnp.abs(v)) * LIN_CODE
            r = jnp.where(v < 0, -r, r)
            v = r if root is True else jnp.where(root, r, v * PHASE_CODE)
        else:
            v = v * PHASE_CODE
        return jnp.round(v).astype(jnp.int32).astype(jnp.int16)

    def encode(n):
        for place in range(8):
            at = (place // 4) * 48
            packed[pl.ds(n, 1), place % 4, at : at + 16, :] = to_code(sums[place, 0:16, :], True)[None]
            packed[pl.ds(n, 1), place % 4, at + 16 : at + 48, :] = to_code(sums[place, 16:48, :], None)[None]
        e = jnp.concatenate([ends_sum[...], jnp.zeros((8, 128), F32)], axis=0)
        e = to_code(e, lanes((16, 128)) < 4)
        for y in range(4):
            packed[pl.ds(n, 1), y, 96:112, :] = e[None]

    def pair_of(n, g):
        mid = (n > 0) & (n < 5)
        return jnp.where(mid, 1 + g, 0), jnp.where(mid, n - 1, jnp.where(n == 0, g, 2 + g))

    def red_copy(n, o):
        to = lax.rem(level + o, 4)
        return pltpu.make_async_remote_copy(
            packed.at[n, to], packed_in.at[n, o - 1], red_send.at[n, o - 1], red_recv.at[n, o - 1],
            device_id=(sta, high * 4 + to), device_id_type=MESH,
        )

    def half_copy(n):
        return pltpu.make_async_remote_copy(
            half.at[n], half_in.at[n], half_send.at[n], half_recv.at[n], device_id=across, device_id_type=MESH
        )

    def gather(n):
        for o in range(1, 4):
            red_copy(n, o).wait_recv()

        def codes(rows, size):
            vs = [packed[pl.ds(n, 1), pl.ds(level, 1), pl.ds(rows, size), :][0, 0]]
            vs += [packed_in[pl.ds(n, 1), o, pl.ds(rows, size), :][0] for o in range(3)]
            return [v.astype(jnp.int32).astype(F32) for v in vs]

        def lin(v):
            return v * jnp.abs(v) * (1.0 / (LIN_CODE * LIN_CODE))

        def total(vs):
            return (vs[0] + vs[1]) + (vs[2] + vs[3])

        e = codes(96, 16)
        e = total([jnp.where(lanes((16, 128)) < 4, lin(v), v * (1.0 / PHASE_CODE)) for v in e])[0:8]
        for dst, part in ((kept, high), (half, 1 - high)):
            at = pl.multiple_of(part * 48, 16)
            dst[pl.ds(n, 1), 0:16, :] = total([lin(v) for v in codes(at, 16)])[None]
            dst[pl.ds(n, 1), 16:48, :] = (total(codes(at + 16, 32)) * (1.0 / PHASE_CODE))[None]
            dst[pl.ds(n, 1), 48:56, :] = e[None]
        half_copy(n).start()

    def count_copy(o):
        return pltpu.make_async_remote_copy(
            counts, counts_in.at[o - 1], count_send.at[o - 1], count_recv.at[o - 1],
            device_id=(sta, at_win(o)), device_id_type=MESH,
        )

    def weighted(lin, pr, pi, count):
        inverse = 1.0 / jnp.maximum(count, 1.0)
        pr, pi = pr * inverse, pi * inverse
        return lin * inverse * (pr * pr + pi * pi)

    def mir_copy(n, g, which, src=stack):
        dst, to = ((mirror, flip), (mirror2, turn))[which]
        return pltpu.make_async_remote_copy(
            src.at[n, g], dst.at[n - 1, g], mir_send.at[n - 1, 2 * g + which], mir_recv.at[n - 1, 2 * g + which],
            device_id=(at_sta(1 + g), to), device_id_type=MESH,
        )

    def pick(v, at):
        return jnp.sum(jnp.where(lane == at, v, 0.0), axis=1, keepdims=True)

    def finish(n):
        half_copy(n).wait_recv()
        v = kept[pl.ds(n, 1)][0] + half_in[pl.ds(n, 1)][0]
        count = count_sum[...]
        ones = []
        for g in (0, 1):
            k, jj = pair_of(n, g)
            ones.append([pick(count, k * 8 + 2 * jj + h) for h in (0, 1)])
            rows = [v[16 * q + 8 * g : 16 * q + 8 * g + 8] for q in range(3)]
            stack[pl.ds(n, 1), g] = weighted(*rows, jnp.where(low, *ones[g]))[None]

        @pl.when((n > 0) & (n < 5))
        def _():
            for g in (0, 1):
                mir_copy(n, g, 0).start()

            @pl.when(win != 0)
            def _():
                for g in (0, 1):
                    mir_copy(n, g, 1).start()

            @pl.when(win == 0)
            def _():
                e = v[48:56]
                for g in (0, 1):
                    t = stack[pl.ds(n, 1), g][0]
                    for h in (0, 1):
                        end = weighted(*[pick(e, 4 * q + 2 * g + h) for q in range(3)], ones[g][h])
                        t = jnp.where(lane == 63 + 64 * h, end, t)
                    stack2[pl.ds(n, 1), g] = t[None]
                    mir_copy(n, g, 1, stack2).start()

    def send(n):
        for o in range(1, 4):
            red_copy(n, o).start()

    def arrive(k, jj):
        @pl.when(k == 1)
        def _():
            for h in (0, 1):
                up_copy(2 * jj + h).wait_recv()

                @pl.when(odd)
                def _():
                    pass_copy(2 * jj + h).start()

        @pl.when(k == 2)
        def _():
            for h in (0, 1):
                two_copy(2 * jj + h).wait_recv()

    def step(n, carry):
        k, jj = pair_of(n, 1)
        arrive(k, jj)
        post(0)
        cross(k, jj)
        product()
        k, jj = pair_of(n + 1, 0)
        arrive(k, jj)
        post(1)
        cross(k, jj)
        product()
        encode(n)
        send(n)

        @pl.when(n == 0)
        def _():
            for m in (1, 2):
                flag_copy(m).wait_recv()
                all_flags[8 * m : 8 * m + 8, :] = flags_in[m - 1]
            counts[...] = lax.dot_general(
                flags[...].astype(BF), all_flags[...].astype(BF), (((1,), (1,)), ((), ())), preferred_element_type=F32
            )
            heard(1)
            tell(2)
            for o in range(1, WIN):
                count_copy(o).start()

        @pl.when(n == 2)
        def _():
            heard(2)
            v = counts[...]
            for o in range(1, WIN):
                count_copy(o).wait_recv()
                v = v + counts_in[o - 1]
            count_sum[...] = v

        @pl.when(n >= 2)
        def _():
            gather(n - 2)

        @pl.when(n >= 4)
        def _():
            finish(n - 4)

        return carry

    cross(0, 0)
    product()
    lax.fori_loop(0, 5, step, 0)
    post(0)
    cross(0, 3)
    product()
    gather(3)
    finish(1)
    post(1)
    encode(5)
    send(5)
    gather(4)
    finish(2)
    finish(3)
    gather(5)
    finish(4)
    finish(5)

    row_id = lax.broadcasted_iota(jnp.int32, (128, 128), 0)
    col_id = lanes((128, 128))
    side, place = col_id // 64, lax.rem(col_id, 64)
    lower = win < 4
    take = side * 64 + jnp.where(lower, 63 - place, place)
    direct = jnp.where(row_id == take, 1.0, 0.0)
    take = side * 64 + jnp.where(lower, 64 - place, place - 1)
    mirrored = jnp.where((row_id == take) & (place != 0), 1.0, 0.0)
    take = side * 64 + jnp.where(turn < 4, 63, 0)
    ending = jnp.where((row_id == take) & (place == 0), 1.0, 0.0)

    def ordered(v, table):
        return jnp.dot(v, table, precision=lax.Precision.HIGHEST, preferred_element_type=F32)

    loads[4].wait()
    keep_all[...] = jnp.zeros_like(keep_all)
    for k in range(5):
        keep_all[:, 8 * k : 8 * k + 8] = keep_in[k].astype(F32)
    keep = keep_all[...]
    v = ordered(stack[...].reshape(96, 128), direct)
    for d in range(12):
        n, g = d // 2, d % 2
        k, jj = (1 + g, n - 1) if 0 < n < 5 else (0, g + (2 if n else 0))
        t = v[8 * d : 8 * d + 8]
        at = (k + 2) * 8 + 2 * jj
        t = t * jnp.where(low, keep[:, at : at + 1], keep[:, at + 1 : at + 2])
        out_ref[pl.ds(at, 8, stride=40), :] = t
        out_ref[pl.ds(at + 1, 8, stride=40), :] = pltpu.roll(t, 64, 1)

    for n in range(1, 5):
        for g in (0, 1):
            for which in (0, 1):
                mir_copy(n, g, which).wait_recv()
    v = ordered(mirror[...].reshape(64, 128), mirrored) + ordered(mirror2[...].reshape(64, 128), ending)
    for n in range(8):
        k, jj = 1 + n % 2, n // 2
        t = v[8 * n : 8 * n + 8]
        at = 2 * jj * 40 + (2 - k) * 8
        spot = lane == (2 - k) * 8 + lax.broadcasted_iota(jnp.int32, (8, 128), 0)
        t = t * jnp.where(low, *[
            jnp.sum(jnp.where(spot, keep[j : j + 1, :], 0.0), axis=1, keepdims=True) for j in (2 * jj, 2 * jj + 1)
        ])
        out_ref[at : at + 8, :] = t
        out_ref[at + 40 : at + 48, :] = pltpu.roll(t, 64, 1)

    for d in (1, 2):
        flag_copy(d).wait_send()
    for j in range(8):
        up_copy(j).wait_send()

    @pl.when(odd)
    def _():
        for j in range(8):
            two_copy(j).wait_send()
            pass_copy(j).wait_send()

    for o in range(1, WIN):
        count_copy(o).wait_send()

    def drain(n, carry):
        for o in range(1, 4):
            red_copy(n, o).wait_send()
        half_copy(n).wait_send()
        return carry

    lax.fori_loop(0, 6, drain, 0)
    for n in range(1, 5):
        for g in (0, 1):
            for which in (0, 1):
                mir_copy(n, g, which).wait_send()


def local(n_sta, traces, gap_mask, pair_mask):
    vmem, dma = pltpu.VMEM, pltpu.SemaphoreType.DMA
    anywhere = pl.BlockSpec(memory_space=pltpu.HBM)
    inside = pl.BlockSpec(memory_space=pltpu.VMEM)
    stacked = pl.pallas_call(
        functools.partial(kernel, n_sta),
        out_shape=jax.ShapeDtypeStruct((320, 128), F32),
        in_specs=[anywhere] * 5,
        out_specs=inside,
        scratch_shapes=[
            vmem((8, 16), jnp.int32),
            vmem((5, 8, 8), jnp.int32),
            vmem((128, 2048), F32),
            vmem((768, 2048), BF),
            vmem((1024, 512), BF),
            vmem((1024, 256), BF),
            vmem((512, 512), F32),
            vmem((512, 512), F32),
            vmem((256, 512), F32),
            vmem((128, 256), F32),
            vmem((128, 256), F32),
            vmem((3, 8, 16, 2048), BF),
            vmem((16, 128, 128), F32),
            vmem((2, 16, 2048), F32),
            vmem((512, 1024), BF),
            vmem((512, 512), F32),
            vmem((4, 128, 128), F32),
            vmem((8, 128), F32),
            vmem((2, 8, 128), F32),
            vmem((8, 128), F32),
            vmem((128, 128), F32),
            vmem((8, 128), F32),
            vmem((7, 8, 128), F32),
            vmem((8, 128), F32),
            vmem((8, 48, 128), F32),
            vmem((8, 128), F32),
            vmem((6, 4, 112, 128), jnp.int16),
            vmem((6, 3, 112, 128), jnp.int16),
            vmem((6, 56, 128), F32),
            vmem((6, 56, 128), F32),
            vmem((6, 56, 128), F32),
            vmem((6, 2, 8, 128), F32),
            vmem((6, 2, 8, 128), F32),
            vmem((4, 2, 8, 128), F32),
            vmem((4, 2, 8, 128), F32),
            pltpu.SemaphoreType.REGULAR((3,)),
            dma((5,)),
            dma((2,)),
            dma((2,)),
            dma((8,)),
            dma((8,)),
            dma((8,)),
            dma((2, 8)),
            dma((7,)),
            dma((7,)),
            dma((6, 3)),
            dma((6, 3)),
            dma((6,)),
            dma((6,)),
            dma((4, 4)),
            dma((4, 4)),
        ],
        compiler_params=pltpu.CompilerParams(
            collective_id=0, has_side_effects=True, vmem_limit_bytes=66600000,
        ),
    )(traces.reshape(128, SAMPLES), gap_mask, jnp.transpose(pair_mask, (1, 0, 2)), jnp.asarray(forward_table()), jnp.asarray(inverse_table()))
    return stacked.reshape(8, 5, 8, 128)[..., :64]


def solution(mesh):
    return jax.shard_map(
        functools.partial(local, mesh.shape["sta"]),
        mesh=mesh,
        in_specs=(P("sta", "win", None), P("sta", "win"), P("sta", None, None)),
        out_specs=P("sta", None, None, "win"),
        check_vma=False,
    )
```

```python
import functools

import jax
import jax.numpy as jnp
import ml_dtypes
import numpy as np
from jax import lax
from jax.experimental import pallas as pl
from jax.experimental.pallas import tpu as pltpu
from jax.sharding import PartitionSpec as P

MESH = pl.DeviceIdType.MESH
SAMPLES = 2048
F = 1024
SB = 8
NW = 16
WIN = 8
ROOT = 0.7071067811865476
BF = jnp.bfloat16
F32 = jnp.float32

LANE = np.arange(128)
LANE_K = (LANE % 8) * 16 + LANE // 8


ORDER = (0, 4, 1, 5, 3, 7, 2, 6)


def class_frequency(r):
    return r + 8 * LANE_K


def forward_table():
    moment = np.arange(256)

    def trig(frequency):
        angle = (moment[:, None] * frequency[None, :] % SAMPLES) * (2.0 * np.pi / SAMPLES)
        return np.cos(angle), np.sin(angle)

    columns = []
    for r in (1, 3, 2):
        ca, sa = trig(class_frequency(r))
        cb, sb = trig(SAMPLES - class_frequency(8 - r))
        columns += [ca, cb, sa, sb]
    for r in (0, 4):
        columns += list(trig(class_frequency(r)))
    rest = np.concatenate(columns, axis=1).astype(np.float32)
    parts = []
    for _ in range(3):
        part = rest.astype(ml_dtypes.bfloat16)
        parts.append(part)
        rest = rest - part.astype(np.float32)
    return np.concatenate(parts, axis=0)


def inverse_table():
    frequency = np.concatenate([class_frequency(r) for r in ORDER])
    lag = np.arange(256)
    sine_lag = np.where(lag == 0, 256, lag)

    def angle(t):
        return (frequency[:, None] * t[None, :] % SAMPLES) * (2.0 * np.pi / SAMPLES)

    both = np.concatenate([np.cos(angle(lag)), np.sin(angle(sine_lag))], axis=1)
    return (both.astype(np.float32) * np.float32(1.0 / 32.0)).astype(ml_dtypes.bfloat16)


LIN_CODE = 1430.0
PHASE_CODE = 2047.0
END_ONE = 1.0 / 32.0
END_RATIO = float(np.float32(ROOT).astype(ml_dtypes.bfloat16))


def lanes(shape):
    return lax.broadcasted_iota(jnp.int32, shape, len(shape) - 1)


def spectrum_parts(res, rows):
    r1, r3, r2, r0, r4 = res

    def get(ref, block, lo, hi):
        return ref[pl.ds(block * 128 + rows, 16), lo:hi]

    real, imag = [None] * 8, [None] * 8

    def both(r, yrc, yrs, yic, yis):
        xr, xi = yrc + yis, yic - yrs
        real[r], imag[r] = xr[:, :128], xi[:, :128]
        real[8 - r], imag[8 - r] = xr[:, 128:], -xi[:, 128:]

    both(
        1,
        get(r1, 0, 0, 256) + ROOT * get(r1, 1, 0, 256),
        get(r1, 0, 256, 512) + ROOT * get(r1, 1, 256, 512),
        -(get(r1, 2, 0, 256) + ROOT * get(r1, 3, 0, 256)),
        -(get(r1, 2, 256, 512) + ROOT * get(r1, 3, 256, 512)),
    )
    both(
        3,
        get(r3, 0, 0, 256) - ROOT * get(r3, 1, 0, 256),
        get(r3, 0, 256, 512) - ROOT * get(r3, 1, 256, 512),
        get(r3, 2, 0, 256) - ROOT * get(r3, 3, 0, 256),
        get(r3, 2, 256, 512) - ROOT * get(r3, 3, 256, 512),
    )
    both(2, get(r2, 0, 0, 256), get(r2, 0, 256, 512), -get(r2, 1, 0, 256), -get(r2, 1, 256, 512))
    for r, ref in ((0, r0), (4, r4)):
        real[r], imag[r] = get(ref, 0, 0, 128), -get(ref, 0, 128, 256)
    return real, imag


def kernel(
    n_sta,
    traces_ref,
    gap_ref,
    keep_ref,
    ftab_ref,
    itab_ref,
    out_ref,
    gap,
    keep_in,
    tr,
    ftab,
    itab,
    folded,
    r1,
    r3,
    r2,
    r0,
    r4,
    white,
    own,
    far,
    lhs,
    res,
    edge,
    flags,
    flags_in,
    keep_all,
    all_flags,
    counts,
    counts_in,
    inverse,
    inverse_end,
    sums,
    ends_sum,
    packed,
    direct_in,
    stack,
    stack2,
    mirror,
    mirror2,
    ready,
    load_sem,
    flag_send,
    flag_recv,
    up_send,
    two_send,
    pass_send,
    white_recv,
    count_send,
    count_recv,
    direct_send,
    direct_recv,
    mir_send,
    mir_recv,
):
    sta = lax.axis_index("sta")
    win = lax.axis_index("win")
    odd = lax.rem(sta, 2) == 1

    def at_sta(d):
        return lax.rem(sta + d + n_sta, n_sta)

    def at_win(o):
        return lax.rem(win + o, WIN)

    loads = [
        pltpu.make_async_copy(traces_ref, tr, load_sem.at[0]),
        pltpu.make_async_copy(ftab_ref, ftab, load_sem.at[1]),
        pltpu.make_async_copy(itab_ref, itab, load_sem.at[2]),
        pltpu.make_async_copy(gap_ref, gap, load_sem.at[3]),
        pltpu.make_async_copy(keep_ref, keep_in, load_sem.at[4]),
    ]
    for load in loads:
        load.start()

    barrier = pltpu.get_barrier_semaphore()
    flip, turn = 7 - win, lax.rem(8 - win, WIN)
    high, level = win // 4, lax.rem(win, 4)
    across = (sta, lax.rem(win + 4, WIN))
    near = [(at_sta(d), win) for d in (-2, -1, 1, 2)]
    near += [(sta, high * 4 + lax.rem(level + d, 4)) for d in (1, 3)]
    near += [across]
    for friend in near:
        pl.semaphore_signal(barrier, inc=1, device_id=friend, device_id_type=MESH)

    def tell(t):
        for friend in near:
            pl.semaphore_signal(ready.at[t], inc=1, device_id=friend, device_id_type=MESH)

    def heard(t):
        pl.semaphore_wait(ready.at[t], len(near))

    flags[...] = jnp.zeros_like(flags)
    all_flags[...] = jnp.zeros_like(all_flags)
    ends_sum[...] = jnp.zeros_like(ends_sum)
    loads[0].wait()
    loads[3].wait()
    flags[:, 0:NW] = gap[...].astype(F32)
    all_flags[0:8, :] = flags[...]

    def fold(s, carry):
        row = pl.multiple_of(s * 16, 16)

        def sign(a):
            v = tr[pl.ds(row, 16), a * 256 : (a + 1) * 256]
            return jnp.where(v > 0, 1.0, 0.0) - jnp.where(v < 0, 1.0, 0.0)

        x = [sign(a) for a in range(8)]
        s04, s15, s26, s37 = [x[a] + x[a + 4] for a in range(4)]
        d04, d15, d26, d37 = [x[a] - x[a + 4] for a in range(4)]
        rows = [d04, d15 - d37, d26, d15 + d37, s04 - s26, s15 - s37]
        even, other = s04 + s26, s15 + s37
        rows += [even + other, even - other]
        for n, v in enumerate(rows):
            folded[pl.ds(pl.multiple_of(n * 128 + row, 16), 16), :] = v.astype(BF)
        return carry

    lax.fori_loop(0, 8, fold, 0)
    loads[1].wait()

    def transform(dst, first, count, column, width):
        y = folded[first * 128 : (first + count) * 128, :]
        y = jnp.concatenate([y, y, y], axis=1)
        dst[...] = jnp.dot(y, ftab[:, column : column + width], preferred_element_type=F32)

    transform(r1, 0, 4, 0, 512)
    transform(r3, 0, 4, 512, 512)
    transform(r2, 4, 2, 1024, 512)
    transform(r0, 6, 1, 1536, 256)
    transform(r4, 7, 1, 1792, 256)


    def flag_copy(d):
        return pltpu.make_async_remote_copy(
            flags, flags_in.at[d - 1], flag_send.at[d - 1], flag_recv.at[d - 1],
            device_id=(at_sta(-d), win), device_id_type=MESH,
        )

    def up_copy(j):
        return pltpu.make_async_remote_copy(
            white.at[0, j], white.at[1, j], up_send.at[j], white_recv.at[0, j],
            device_id=(at_sta(-1), win), device_id_type=MESH,
        )

    def two_copy(j):
        return pltpu.make_async_remote_copy(
            white.at[0, j], white.at[2, j], two_send.at[j], white_recv.at[1, j],
            device_id=(at_sta(-2), win), device_id_type=MESH,
        )

    def pass_copy(j):
        return pltpu.make_async_remote_copy(
            white.at[1, j], white.at[2, j], pass_send.at[j], white_recv.at[1, j],
            device_id=(at_sta(-1), win), device_id_type=MESH,
        )

    def whiten(s, carry):
        row = pl.multiple_of(s * 16, 16)
        real, imag = spectrum_parts((r1, r3, r2, r0, r4), row)
        power = real[0] * real[0] + imag[0] * imag[0]
        for r in range(1, 8):
            power = power + (real[r] * real[r] + imag[r] * imag[r])
        for shift in (8, 16, 32, 64):
            power = power + pltpu.roll(power, shift, 1)
        band = power * (1.0 / 128.0)
        flag = jnp.broadcast_to(flags[pl.ds(s, 1), :], (16, 128))
        eye = lanes((16, 128)) == lax.broadcasted_iota(jnp.int32, (16, 128), 0)
        flag = jnp.sum(jnp.where(eye, flag, 0.0), axis=1, keepdims=True)
        factor = 1.0 / jnp.sqrt(band + 1e-05) * flag
        for r in range(8):
            for half, v in ((0, real[r]), (1024, imag[r])):
                v = (v * factor).astype(BF)
                c = half + r * 128
                white[0, pl.ds(s, 1), :, c : c + 128] = v[None]
                own[c // 128, pl.ds(s, 16, stride=8), :] = v.astype(F32)
        up_copy(s).start()

        @pl.when(odd)
        def _():
            two_copy(s).start()

        return carry

    pl.semaphore_wait(barrier, len(near))
    lax.fori_loop(0, 8, whiten, 0)
    tell(0)
    for d in (1, 2):
        flag_copy(d).start()
    loads[2].wait()
    loads[4].wait()

    lane = lanes((8, 128))
    first_lane = lane == 0
    low = lane < 64

    def cross(k, jj):
        for h in (0, 1):
            far[h] = white[pl.ds(k, 1), pl.ds(2 * jj + h, 1)][0, 0].astype(F32)
        for m in range(4):
            for wp in range(8):
                rows = slice(16 * wp, 16 * wp + 16)
                ends = [None] * 4
                for p in (2 * m, 2 * m + 1):
                    r = ORDER[p]
                    ar, ai = own[r, rows, :], own[8 + r, rows, :]
                    for h in (0, 1):

                        def spread(r):
                            c = slice(128 * r, 128 * r + 128)
                            return jnp.concatenate(
                                [jnp.broadcast_to(far[h, 2 * wp + g : 2 * wp + g + 1, c], (8, 128)) for g in (0, 1)],
                                axis=0,
                            )

                        br, bi = spread(r), spread(8 + r)
                        for which, v in ((0, ar * br + ai * bi), (1, ai * br - ar * bi)):
                            at = h * 256 + which * 128 + 16 * wp
                            lhs[at : at + 16, 128 * p : 128 * p + 128] = v.astype(BF)
                            n = 2 * h + which
                            if m < 3:
                                plus = r in (0, 1, 7)
                                ends[n] = v if ends[n] is None else (ends[n] - v if not plus else v - ends[n])
                for n in range(4):
                    if m == 0:
                        edge[n, rows, :] = ends[n]
                    elif m == 1:
                        edge[n, rows, :] = edge[n, rows, :] + END_RATIO * ends[n]
                    elif m == 2:
                        v = edge[n, rows, :] + END_RATIO * ends[n]
                        v = jnp.sum(v * END_ONE, axis=1, keepdims=True)
                        edge[n, rows, :] = jnp.broadcast_to(v, (16, 128))

    def product():
        res[...] = jnp.dot(lhs[...], itab[...], preferred_element_type=F32)

    def collect(h):
        zero = jnp.zeros((8, 128), F32)
        total = [[zero] * 3 for _ in range(4)]
        end_re, end_im = zero, zero

        def parts(re, im):
            scale = lax.rsqrt(jnp.maximum(re * re + im * im, 0.25))
            return re, re * scale, im * scale

        def add(n, re, im):
            total[n] = [t + v for t, v in zip(total[n], parts(re, im))]

        for w in range(NW):
            wr = slice(8 * w, 8 * w + 8)
            re_rows = slice(256 * h + 8 * w, 256 * h + 8 * w + 8)
            im_rows = slice(256 * h + 128 + 8 * w, 256 * h + 136 + 8 * w)
            for tile in range(2):
                cos, sin = slice(128 * tile, 128 * tile + 128), slice(256 + 128 * tile, 384 + 128 * tile)
                a, c = res[re_rows, cos], res[re_rows, sin]
                d, b = res[im_rows, cos], res[im_rows, sin]
                if tile == 0:
                    edge_re, edge_im = edge[2 * h, wr, :], edge[2 * h + 1, wr, :]
                    add(0, a - jnp.where(first_lane, 0.0, b), d + jnp.where(first_lane, 0.0, c))
                    a, d = jnp.where(first_lane, edge_re, a), jnp.where(first_lane, edge_im, d)
                    x, y = a - b, d + c
                    if w:
                        x, y = pltpu.roll(x, w, 1), pltpu.roll(y, w, 1)
                    end_re, end_im = jnp.where(lane == w, x, end_re), jnp.where(lane == w, y, end_im)
                else:
                    add(1, a - b, d + c)
                add(2 + tile, a + b, d - c)
        end = [jnp.sum(v, axis=1, keepdims=True) for v in parts(end_re, end_im)]
        out = []
        for q in range(3):
            neg = pltpu.roll(jnp.concatenate([total[2][q], total[3][q]], axis=1), 255, 1)
            out.append([total[0][q], total[1][q], neg[:, :128], neg[:, 128:], end[q]])
        return out

    def post(g):
        one, two = collect(0), collect(1)
        for q in range(3):
            rows = slice(16 * q + 8 * g, 16 * q + 8 * g + 8)
            for n in range(4):
                x, y = one[q][n], two[q][n]
                left = jnp.where(low, x, pltpu.roll(y, 64, 1))
                right = jnp.where(low, pltpu.roll(x, 64, 1), y)
                if n < 2:
                    places = (4 + 2 * n, 5 + 2 * n)
                else:
                    places = (3 - 2 * (n - 2), 2 - 2 * (n - 2))
                for place, v in zip(places, (left, right)):
                    sums[place, rows, :] = v
            e = jnp.where(lane == 4 * q + 2 * g, one[q][3 + 1], ends_sum[...])
            ends_sum[...] = jnp.where(lane == 4 * q + 2 * g + 1, two[q][4], e)

    def to_code(v, root):
        if root is not None:
            r = jnp.sqrt(jnp.abs(v)) * LIN_CODE
            r = jnp.where(v < 0, -r, r)
            v = r if root is True else jnp.where(root, r, v * PHASE_CODE)
        else:
            v = v * PHASE_CODE
        return jnp.round(v).astype(jnp.int32).astype(jnp.int16)

    def encode(n):
        for place in range(8):
            at = (place // 4) * 64
            packed[pl.ds(n, 1), place % 4, at : at + 16, :] = to_code(sums[place, 0:16, :], True)[None]
            packed[pl.ds(n, 1), place % 4, at + 16 : at + 48, :] = to_code(sums[place, 16:48, :], None)[None]
        e = jnp.concatenate([ends_sum[...], jnp.zeros((8, 128), F32)], axis=0)
        e = to_code(e, lanes((16, 128)) < 4)
        for y in range(4):
            for at in (48, 112):
                packed[pl.ds(n, 1), y, at : at + 16, :] = e[None]

    def pair_of(n, g):
        mid = (n > 0) & (n < 5)
        return jnp.where(mid, 1 + g, 0), jnp.where(mid, n - 1, jnp.where(n == 0, g, 2 + g))

    def direct_copy(n, o):
        to = at_win(o)
        return pltpu.make_async_remote_copy(
            packed.at[n, lax.rem(to, 4), pl.ds(pl.multiple_of((to // 4) * 64, 64), 64)],
            direct_in.at[n, o - 1], direct_send.at[n, o - 1], direct_recv.at[n, o - 1],
            device_id=(sta, to), device_id_type=MESH,
        )

    def lin(v):
        return v * jnp.abs(v) * (1.0 / (LIN_CODE * LIN_CODE))

    def wide(v):
        return v.astype(jnp.int32).astype(F32)

    def added(vs):
        while len(vs) > 1:
            vs = [sum(vs[i : i + 2]) for i in range(0, len(vs), 2)]
        return vs[0]

    def decoded(read):
        first = added([lin(wide(v)) for v in read(0, 16)])
        rest = added([wide(v) for v in read(16, 32)]) * (1.0 / PHASE_CODE)
        end = [wide(v) for v in read(48, 16)]
        end = added([jnp.where(lanes((16, 128)) < 4, lin(v), v * (1.0 / PHASE_CODE)) for v in end])
        return first, rest, end[0:8]

    def count_copy(o):
        return pltpu.make_async_remote_copy(
            counts, counts_in.at[o - 1], count_send.at[o - 1], count_recv.at[o - 1],
            device_id=(sta, at_win(o)), device_id_type=MESH,
        )

    def weighted(lin, pr, pi, inv):
        pr, pi = pr * inv, pi * inv
        return lin * inv * (pr * pr + pi * pi)

    def mir_copy(n, g, which, src=stack):
        dst, to = ((mirror, flip), (mirror2, turn))[which]
        return pltpu.make_async_remote_copy(
            src.at[n, g], dst.at[n - 1, g], mir_send.at[n - 1, 2 * g + which], mir_recv.at[n - 1, 2 * g + which],
            device_id=(at_sta(1 + g), to), device_id_type=MESH,
        )

    def finish(n):
        for o in range(1, WIN):
            direct_copy(n, o).wait_recv()

        def read(row, size):
            at = pl.ds(pl.multiple_of(high * 64 + row, 16), size)
            vs = [packed[pl.ds(n, 1), pl.ds(level, 1), at, :][0, 0]]
            return vs + [direct_in[pl.ds(n, 1), o, row : row + size, :][0] for o in range(7)]

        conclude(n, jnp.concatenate(decoded(read), axis=0))

    def conclude(n, v):
        for g in (0, 1):
            rows = [v[16 * q + 8 * g : 16 * q + 8 * g + 8] for q in range(3)]
            stack[pl.ds(n, 1), g] = weighted(*rows, inverse[pl.ds(n, 1), g][0])[None]

        @pl.when((n > 0) & (n < 5))
        def _():
            for g in (0, 1):
                mir_copy(n, g, 0).start()

            @pl.when(win != 0)
            def _():
                for g in (0, 1):
                    mir_copy(n, g, 1).start()

            @pl.when(win == 0)
            def _():
                e = v[48:56]
                end = weighted(e, pltpu.roll(e, 124, 1), pltpu.roll(e, 120, 1), inverse_end[pl.ds(n, 1)][0])
                for g in (0, 1):
                    t = stack[pl.ds(n, 1), g][0]
                    for h in (0, 1):
                        t = jnp.where(lane == 63 + 64 * h, end[:, 2 * g + h : 2 * g + h + 1], t)
                    stack2[pl.ds(n, 1), g] = t[None]
                    mir_copy(n, g, 1, stack2).start()

    def send(n):
        for o in range(1, WIN):
            direct_copy(n, o).start()

    def arrive(k, jj):
        @pl.when(k == 1)
        def _():
            for h in (0, 1):
                up_copy(2 * jj + h).wait_recv()

                @pl.when(odd)
                def _():
                    pass_copy(2 * jj + h).start()

        @pl.when(k == 2)
        def _():
            for h in (0, 1):
                two_copy(2 * jj + h).wait_recv()

    def step(n, carry):
        k, jj = pair_of(n, 1)
        arrive(k, jj)
        post(0)
        cross(k, jj)
        product()
        k, jj = pair_of(n + 1, 0)
        arrive(k, jj)
        post(1)
        cross(k, jj)
        product()
        encode(n)

        @pl.when(n == 0)
        def _():
            heard(0)
            tell(1)

        @pl.when(n == 1)
        def _():
            heard(1)
            tell(2)
            send(0)

        @pl.when(n >= 1)
        def _():
            send(n)

        @pl.when(n == 1)
        def _():
            for m in (1, 2):
                flag_copy(m).wait_recv()
                all_flags[8 * m : 8 * m + 8, :] = flags_in[m - 1]
            counts[...] = lax.dot_general(
                flags[...].astype(BF), all_flags[...].astype(BF), (((1,), (1,)), ((), ())), preferred_element_type=F32
            )
            for o in range(1, WIN):
                count_copy(o).start()

        @pl.when(n == 4)
        def _():
            heard(2)
            v = counts[...]
            for o in range(1, WIN):
                count_copy(o).wait_recv()
                v = v + counts_in[o - 1]
            v = 1.0 / jnp.maximum(v, 1.0)
            for m in range(6):
                end = jnp.ones((8, 128), F32)
                for g in (0, 1):
                    k, jj = (1 + g, m - 1) if 0 < m < 5 else (0, g + (2 if m else 0))
                    two = [v[:, k * 8 + 2 * jj + h : k * 8 + 2 * jj + h + 1] for h in (0, 1)]
                    inverse[m, g] = jnp.where(low, *two)
                    for h in (0, 1):
                        end = jnp.where(lane == 2 * g + h, two[h], end)
                inverse_end[m] = end

        @pl.when(n == 4)
        def _():
            for m in range(3):
                finish(m)

        return carry

    cross(0, 0)
    product()
    lax.fori_loop(0, 5, step, 0)
    post(0)
    cross(0, 3)
    product()
    finish(3)
    post(1)
    encode(5)
    send(5)
    finish(4)
    row_id = lax.broadcasted_iota(jnp.int32, (128, 128), 0)
    col_id = lanes((128, 128))
    side, place = col_id // 64, lax.rem(col_id, 64)
    lower = win < 4
    take = side * 64 + jnp.where(lower, 63 - place, place)
    direct = jnp.where(row_id == take, 1.0, 0.0)
    take = side * 64 + jnp.where(lower, 64 - place, place - 1)
    mirrored = jnp.where((row_id == take) & (place != 0), 1.0, 0.0)
    take = side * 64 + jnp.where(turn < 4, 63, 0)
    ending = jnp.where((row_id == take) & (place == 0), 1.0, 0.0)

    def ordered(v, table):
        return jnp.dot(v, table, precision=lax.Precision.HIGHEST, preferred_element_type=F32)

    keep_all[...] = jnp.zeros_like(keep_all)
    for k in range(5):
        keep_all[:, 8 * k : 8 * k + 8] = keep_in[k].astype(F32)
    keep = keep_all[...]
    masks = []
    for n in range(8):
        k, jj = 1 + n % 2, n // 2
        spot = lane == (2 - k) * 8 + lax.broadcasted_iota(jnp.int32, (8, 128), 0)
        masks.append(jnp.where(low, *[
            jnp.sum(jnp.where(spot, keep[j : j + 1, :], 0.0), axis=1, keepdims=True) for j in (2 * jj, 2 * jj + 1)
        ]))
    finish(5)

    v = ordered(stack[...].reshape(96, 128), direct)
    for d in range(12):
        n, g = d // 2, d % 2
        k, jj = (1 + g, n - 1) if 0 < n < 5 else (0, g + (2 if n else 0))
        t = v[8 * d : 8 * d + 8]
        at = (k + 2) * 8 + 2 * jj
        t = t * jnp.where(low, keep[:, at : at + 1], keep[:, at + 1 : at + 2])
        out_ref[pl.ds(at, 8, stride=40), :] = t
        out_ref[pl.ds(at + 1, 8, stride=40), :] = pltpu.roll(t, 64, 1)

    for n in range(1, 5):
        for g in (0, 1):
            for which in (0, 1):
                mir_copy(n, g, which).wait_recv()
    v = ordered(mirror[...].reshape(64, 128), mirrored) + ordered(mirror2[...].reshape(64, 128), ending)
    for n in range(8):
        k, jj = 1 + n % 2, n // 2
        t = v[8 * n : 8 * n + 8]
        at = 2 * jj * 40 + (2 - k) * 8
        t = t * masks[n]
        out_ref[at : at + 8, :] = t
        out_ref[at + 40 : at + 48, :] = pltpu.roll(t, 64, 1)

    for d in (1, 2):
        flag_copy(d).wait_send()
    for j in range(8):
        up_copy(j).wait_send()

    @pl.when(odd)
    def _():
        for j in range(8):
            two_copy(j).wait_send()
            pass_copy(j).wait_send()

    for o in range(1, WIN):
        count_copy(o).wait_send()

    def drain(n, carry):
        for o in range(1, WIN):
            direct_copy(n, o).wait_send()
        return carry

    lax.fori_loop(0, 6, drain, 0)
    for n in range(1, 5):
        for g in (0, 1):
            for which in (0, 1):
                mir_copy(n, g, which).wait_send()


def local(n_sta, traces, gap_mask, pair_mask):
    vmem, dma = pltpu.VMEM, pltpu.SemaphoreType.DMA
    anywhere = pl.BlockSpec(memory_space=pltpu.HBM)
    inside = pl.BlockSpec(memory_space=pltpu.VMEM)
    stacked = pl.pallas_call(
        functools.partial(kernel, n_sta),
        out_shape=jax.ShapeDtypeStruct((320, 128), F32),
        in_specs=[anywhere] * 5,
        out_specs=inside,
        scratch_shapes=[
            vmem((8, 16), jnp.int32),
            vmem((5, 8, 8), jnp.int32),
            vmem((128, 2048), F32),
            vmem((768, 2048), BF),
            vmem((1024, 512), BF),
            vmem((1024, 256), BF),
            vmem((512, 512), F32),
            vmem((512, 512), F32),
            vmem((256, 512), F32),
            vmem((128, 256), F32),
            vmem((128, 256), F32),
            vmem((3, 8, 16, 2048), BF),
            vmem((16, 128, 128), F32),
            vmem((2, 16, 2048), F32),
            vmem((512, 1024), BF),
            vmem((512, 512), F32),
            vmem((4, 128, 128), F32),
            vmem((8, 128), F32),
            vmem((2, 8, 128), F32),
            vmem((8, 128), F32),
            vmem((128, 128), F32),
            vmem((8, 128), F32),
            vmem((7, 8, 128), F32),
            vmem((6, 2, 8, 128), F32),
            vmem((6, 8, 128), F32),
            vmem((8, 48, 128), F32),
            vmem((8, 128), F32),
            vmem((6, 4, 128, 128), jnp.int16),
            vmem((6, 7, 64, 128), jnp.int16),
            vmem((6, 2, 8, 128), F32),
            vmem((6, 2, 8, 128), F32),
            vmem((4, 2, 8, 128), F32),
            vmem((4, 2, 8, 128), F32),
            pltpu.SemaphoreType.REGULAR((3,)),
            dma((5,)),
            dma((2,)),
            dma((2,)),
            dma((8,)),
            dma((8,)),
            dma((8,)),
            dma((2, 8)),
            dma((7,)),
            dma((7,)),
            dma((6, 7)),
            dma((6, 7)),
            dma((4, 4)),
            dma((4, 4)),
        ],
        compiler_params=pltpu.CompilerParams(
            collective_id=0, has_side_effects=True, vmem_limit_bytes=66600000,
        ),
    )(traces.reshape(128, SAMPLES), gap_mask, jnp.transpose(pair_mask, (1, 0, 2)), jnp.asarray(forward_table()), jnp.asarray(inverse_table()))
    return stacked.reshape(8, 5, 8, 128)[..., :64]


def solution(mesh):
    return jax.shard_map(
        functools.partial(local, mesh.shape["sta"]),
        mesh=mesh,
        in_specs=(P("sta", "win", None), P("sta", "win"), P("sta", None, None)),
        out_specs=P("sta", None, None, "win"),
        check_vma=False,
    )
```

```python
import functools

import jax
import jax.numpy as jnp
import ml_dtypes
import numpy as np
from jax import lax
from jax.experimental import pallas as pl
from jax.experimental.pallas import tpu as pltpu
from jax.sharding import PartitionSpec as P

MESH = pl.DeviceIdType.MESH
SAMPLES = 2048
F = 1024
SB = 8
NW = 16
WIN = 8
ROOT = 0.7071067811865476
BF = jnp.bfloat16
F32 = jnp.float32

LANE = np.arange(128)
LANE_K = (LANE % 8) * 16 + LANE // 8


ORDER = (0, 4, 1, 5, 3, 7, 2, 6)


def class_frequency(r):
    return r + 8 * LANE_K


def forward_table():
    moment = np.arange(256)

    def trig(frequency):
        angle = (moment[:, None] * frequency[None, :] % SAMPLES) * (2.0 * np.pi / SAMPLES)
        return np.cos(angle), np.sin(angle)

    columns = []
    for r in (1, 3, 2):
        ca, sa = trig(class_frequency(r))
        cb, sb = trig(SAMPLES - class_frequency(8 - r))
        columns += [ca, cb, sa, sb]
    for r in (0, 4):
        columns += list(trig(class_frequency(r)))
    rest = np.concatenate(columns, axis=1).astype(np.float32)
    parts = []
    for _ in range(3):
        part = rest.astype(ml_dtypes.bfloat16)
        parts.append(part)
        rest = rest - part.astype(np.float32)
    return np.concatenate(parts, axis=0)


def inverse_table():
    frequency = np.concatenate([class_frequency(r) for r in ORDER])
    lag = np.arange(256)
    sine_lag = np.where(lag == 0, 256, lag)

    def angle(t):
        return (frequency[:, None] * t[None, :] % SAMPLES) * (2.0 * np.pi / SAMPLES)

    both = np.concatenate([np.cos(angle(lag)), np.sin(angle(sine_lag))], axis=1)
    return (both.astype(np.float32) * np.float32(1.0 / 32.0)).astype(ml_dtypes.bfloat16)


LIN_CODE = 1430.0
PHASE_CODE = 2047.0
END_ONE = 1.0 / 32.0
END_RATIO = float(np.float32(ROOT).astype(ml_dtypes.bfloat16))


def lanes(shape):
    return lax.broadcasted_iota(jnp.int32, shape, len(shape) - 1)


def spectrum_parts(res, rows):
    r1, r3, r2, r0, r4 = res

    def get(ref, block, lo, hi):
        return ref[pl.ds(block * 128 + rows, 16), lo:hi]

    real, imag = [None] * 8, [None] * 8

    def both(r, yrc, yrs, yic, yis):
        xr, xi = yrc + yis, yic - yrs
        real[r], imag[r] = xr[:, :128], xi[:, :128]
        real[8 - r], imag[8 - r] = xr[:, 128:], -xi[:, 128:]

    both(
        1,
        get(r1, 0, 0, 256) + ROOT * get(r1, 1, 0, 256),
        get(r1, 0, 256, 512) + ROOT * get(r1, 1, 256, 512),
        -(get(r1, 2, 0, 256) + ROOT * get(r1, 3, 0, 256)),
        -(get(r1, 2, 256, 512) + ROOT * get(r1, 3, 256, 512)),
    )
    both(
        3,
        get(r3, 0, 0, 256) - ROOT * get(r3, 1, 0, 256),
        get(r3, 0, 256, 512) - ROOT * get(r3, 1, 256, 512),
        get(r3, 2, 0, 256) - ROOT * get(r3, 3, 0, 256),
        get(r3, 2, 256, 512) - ROOT * get(r3, 3, 256, 512),
    )
    both(2, get(r2, 0, 0, 256), get(r2, 0, 256, 512), -get(r2, 1, 0, 256), -get(r2, 1, 256, 512))
    for r, ref in ((0, r0), (4, r4)):
        real[r], imag[r] = get(ref, 0, 0, 128), -get(ref, 0, 128, 256)
    return real, imag


def kernel(
    n_sta,
    traces_ref,
    gap_ref,
    keep_ref,
    ftab_ref,
    itab_ref,
    out_ref,
    gap,
    keep_in,
    tr,
    ftab,
    itab,
    folded,
    r1,
    r3,
    r2,
    r0,
    r4,
    white,
    own,
    far,
    lhs,
    res,
    edge,
    flags,
    flags_in,
    keep_all,
    all_flags,
    counts,
    counts_in,
    inverse,
    inverse_end,
    sums,
    ends_sum,
    packed,
    direct_in,
    stack,
    stack2,
    mirror,
    mirror2,
    ready,
    load_sem,
    flag_send,
    flag_recv,
    up_send,
    two_send,
    pass_send,
    white_recv,
    count_send,
    count_recv,
    direct_send,
    direct_recv,
    mir_send,
    mir_recv,
):
    sta = lax.axis_index("sta")
    win = lax.axis_index("win")
    odd = lax.rem(sta, 2) == 1

    def at_sta(d):
        return lax.rem(sta + d + n_sta, n_sta)

    def at_win(o):
        return lax.rem(win + o, WIN)

    loads = [
        pltpu.make_async_copy(traces_ref, tr, load_sem.at[0]),
        pltpu.make_async_copy(ftab_ref, ftab, load_sem.at[1]),
        pltpu.make_async_copy(itab_ref, itab, load_sem.at[2]),
        pltpu.make_async_copy(gap_ref, gap, load_sem.at[3]),
        pltpu.make_async_copy(keep_ref, keep_in, load_sem.at[4]),
    ]
    for load in loads:
        load.start()

    barrier = pltpu.get_barrier_semaphore()
    flip, turn = 7 - win, lax.rem(8 - win, WIN)
    high, level = win // 4, lax.rem(win, 4)
    across = (sta, lax.rem(win + 4, WIN))
    near = [(at_sta(d), win) for d in (-2, -1, 1, 2)]
    near += [(sta, high * 4 + lax.rem(level + d, 4)) for d in (1, 3)]
    near += [across]
    for friend in near:
        pl.semaphore_signal(barrier, inc=1, device_id=friend, device_id_type=MESH)

    def tell(t):
        for friend in near:
            pl.semaphore_signal(ready.at[t], inc=1, device_id=friend, device_id_type=MESH)

    def heard(t):
        pl.semaphore_wait(ready.at[t], len(near))

    flags[...] = jnp.zeros_like(flags)
    all_flags[...] = jnp.zeros_like(all_flags)
    ends_sum[...] = jnp.zeros_like(ends_sum)
    loads[0].wait()
    loads[3].wait()
    flags[:, 0:NW] = gap[...].astype(F32)
    all_flags[0:8, :] = flags[...]

    def fold(s, carry):
        row = pl.multiple_of(s * 16, 16)

        def sign(a):
            v = tr[pl.ds(row, 16), a * 256 : (a + 1) * 256]
            return jnp.where(v > 0, 1.0, 0.0) - jnp.where(v < 0, 1.0, 0.0)

        x = [sign(a) for a in range(8)]
        s04, s15, s26, s37 = [x[a] + x[a + 4] for a in range(4)]
        d04, d15, d26, d37 = [x[a] - x[a + 4] for a in range(4)]
        rows = [d04, d15 - d37, d26, d15 + d37, s04 - s26, s15 - s37]
        even, other = s04 + s26, s15 + s37
        rows += [even + other, even - other]
        for n, v in enumerate(rows):
            folded[pl.ds(pl.multiple_of(n * 128 + row, 16), 16), :] = v.astype(BF)
        return carry

    lax.fori_loop(0, 8, fold, 0)
    loads[1].wait()

    def transform(dst, first, count, column, width):
        y = folded[first * 128 : (first + count) * 128, :]
        y = jnp.concatenate([y, y, y], axis=1)
        dst[...] = jnp.dot(y, ftab[:, column : column + width], preferred_element_type=F32)

    transform(r1, 0, 4, 0, 512)
    transform(r3, 0, 4, 512, 512)
    transform(r2, 4, 2, 1024, 512)
    transform(r0, 6, 1, 1536, 256)
    transform(r4, 7, 1, 1792, 256)


    def flag_copy(d):
        return pltpu.make_async_remote_copy(
            flags, flags_in.at[d - 1], flag_send.at[d - 1], flag_recv.at[d - 1],
            device_id=(at_sta(-d), win), device_id_type=MESH,
        )

    def up_copy(j):
        return pltpu.make_async_remote_copy(
            white.at[0, j], white.at[1, j], up_send.at[j], white_recv.at[0, j],
            device_id=(at_sta(-1), win), device_id_type=MESH,
        )

    def two_copy(j):
        return pltpu.make_async_remote_copy(
            white.at[0, j], white.at[2, j], two_send.at[j], white_recv.at[1, j],
            device_id=(at_sta(-2), win), device_id_type=MESH,
        )

    def pass_copy(j):
        return pltpu.make_async_remote_copy(
            white.at[1, j], white.at[2, j], pass_send.at[j], white_recv.at[1, j],
            device_id=(at_sta(-1), win), device_id_type=MESH,
        )

    def whiten(s, carry):
        row = pl.multiple_of(s * 16, 16)
        real, imag = spectrum_parts((r1, r3, r2, r0, r4), row)
        power = real[0] * real[0] + imag[0] * imag[0]
        for r in range(1, 8):
            power = power + (real[r] * real[r] + imag[r] * imag[r])
        for shift in (8, 16, 32, 64):
            power = power + pltpu.roll(power, shift, 1)
        band = power * (1.0 / 128.0)
        flag = jnp.broadcast_to(flags[pl.ds(s, 1), :], (16, 128))
        eye = lanes((16, 128)) == lax.broadcasted_iota(jnp.int32, (16, 128), 0)
        flag = jnp.sum(jnp.where(eye, flag, 0.0), axis=1, keepdims=True)
        factor = 1.0 / jnp.sqrt(band + 1e-05) * flag
        for r in range(8):
            for half, v in ((0, real[r]), (1024, imag[r])):
                v = (v * factor).astype(BF)
                c = half + r * 128
                white[0, pl.ds(s, 1), :, c : c + 128] = v[None]
                own[c // 128, pl.ds(s, 16, stride=8), :] = v.astype(F32)
        up_copy(s).start()

        @pl.when(odd)
        def _():
            two_copy(s).start()

        return carry

    pl.semaphore_wait(barrier, len(near))
    lax.fori_loop(0, 8, whiten, 0)
    tell(0)
    for d in (1, 2):
        flag_copy(d).start()
    loads[2].wait()
    loads[4].wait()

    lane = lanes((8, 128))
    first_lane = lane == 0
    low = lane < 64

    def cross(k, jj):
        for h in (0, 1):
            far[h] = white[pl.ds(k, 1), pl.ds(2 * jj + h, 1)][0, 0].astype(F32)
        for m in range(4):
            for wp in range(8):
                rows = slice(16 * wp, 16 * wp + 16)
                ends = [None] * 4
                for p in (2 * m, 2 * m + 1):
                    r = ORDER[p]
                    ar, ai = own[r, rows, :], own[8 + r, rows, :]
                    for h in (0, 1):

                        def spread(r):
                            c = slice(128 * r, 128 * r + 128)
                            return jnp.concatenate(
                                [jnp.broadcast_to(far[h, 2 * wp + g : 2 * wp + g + 1, c], (8, 128)) for g in (0, 1)],
                                axis=0,
                            )

                        br, bi = spread(r), spread(8 + r)
                        for which, v in ((0, ar * br + ai * bi), (1, ai * br - ar * bi)):
                            at = h * 256 + which * 128 + 16 * wp
                            lhs[at : at + 16, 128 * p : 128 * p + 128] = v.astype(BF)
                            n = 2 * h + which
                            if m < 3:
                                plus = r in (0, 1, 7)
                                ends[n] = v if ends[n] is None else (ends[n] - v if not plus else v - ends[n])
                for n in range(4):
                    if m == 0:
                        edge[n, rows, :] = ends[n]
                    elif m == 1:
                        edge[n, rows, :] = edge[n, rows, :] + END_RATIO * ends[n]
                    elif m == 2:
                        v = edge[n, rows, :] + END_RATIO * ends[n]
                        v = jnp.sum(v * END_ONE, axis=1, keepdims=True)
                        edge[n, rows, :] = jnp.broadcast_to(v, (16, 128))

    def product():
        res[...] = jnp.dot(lhs[...], itab[...], preferred_element_type=F32)

    def collect(h):
        zero = jnp.zeros((8, 128), F32)
        total = [[zero] * 3 for _ in range(4)]
        end_re, end_im = zero, zero

        def parts(re, im):
            scale = lax.rsqrt(jnp.maximum(re * re + im * im, 0.25))
            return re, re * scale, im * scale

        def add(n, re, im):
            total[n] = [t + v for t, v in zip(total[n], parts(re, im))]

        for w in range(NW):
            wr = slice(8 * w, 8 * w + 8)
            re_rows = slice(256 * h + 8 * w, 256 * h + 8 * w + 8)
            im_rows = slice(256 * h + 128 + 8 * w, 256 * h + 136 + 8 * w)
            for tile in range(2):
                cos, sin = slice(128 * tile, 128 * tile + 128), slice(256 + 128 * tile, 384 + 128 * tile)
                a, c = res[re_rows, cos], res[re_rows, sin]
                d, b = res[im_rows, cos], res[im_rows, sin]
                if tile == 0:
                    edge_re, edge_im = edge[2 * h, wr, :], edge[2 * h + 1, wr, :]
                    add(0, a - jnp.where(first_lane, 0.0, b), d + jnp.where(first_lane, 0.0, c))
                    a, d = jnp.where(first_lane, edge_re, a), jnp.where(first_lane, edge_im, d)
                    x, y = a - b, d + c
                    if w:
                        x, y = pltpu.roll(x, w, 1), pltpu.roll(y, w, 1)
                    end_re, end_im = jnp.where(lane == w, x, end_re), jnp.where(lane == w, y, end_im)
                else:
                    add(1, a - b, d + c)
                add(2 + tile, a + b, d - c)
        end = [jnp.sum(v, axis=1, keepdims=True) for v in parts(end_re, end_im)]
        out = []
        for q in range(3):
            neg = pltpu.roll(jnp.concatenate([total[2][q], total[3][q]], axis=1), 255, 1)
            out.append([total[0][q], total[1][q], neg[:, :128], neg[:, 128:], end[q]])
        return out

    def post(g):
        one, two = collect(0), collect(1)
        for q in range(3):
            rows = slice(16 * q + 8 * g, 16 * q + 8 * g + 8)
            for n in range(4):
                x, y = one[q][n], two[q][n]
                left = jnp.where(low, x, pltpu.roll(y, 64, 1))
                right = jnp.where(low, pltpu.roll(x, 64, 1), y)
                if n < 2:
                    places = (4 + 2 * n, 5 + 2 * n)
                else:
                    places = (3 - 2 * (n - 2), 2 - 2 * (n - 2))
                for place, v in zip(places, (left, right)):
                    sums[place, rows, :] = v
            e = jnp.where(lane == 4 * q + 2 * g, one[q][3 + 1], ends_sum[...])
            ends_sum[...] = jnp.where(lane == 4 * q + 2 * g + 1, two[q][4], e)

    def to_code(v, root):
        if root is not None:
            r = jnp.sqrt(jnp.abs(v)) * LIN_CODE
            r = jnp.where(v < 0, -r, r)
            v = r if root is True else jnp.where(root, r, v * PHASE_CODE)
        else:
            v = v * PHASE_CODE
        return jnp.round(v).astype(jnp.int32).astype(jnp.int16)

    def encode(n):
        for place in range(8):
            at = (place // 4) * 64
            packed[pl.ds(n, 1), place % 4, at : at + 16, :] = to_code(sums[place, 0:16, :], True)[None]
            packed[pl.ds(n, 1), place % 4, at + 16 : at + 48, :] = to_code(sums[place, 16:48, :], None)[None]
        e = jnp.concatenate([ends_sum[...], jnp.zeros((8, 128), F32)], axis=0)
        e = to_code(e, lanes((16, 128)) < 4)
        for y in range(4):
            for at in (48, 112):
                packed[pl.ds(n, 1), y, at : at + 16, :] = e[None]

    def pair_of(n, g):
        mid = (n > 0) & (n < 5)
        return jnp.where(mid, 1 + g, 0), jnp.where(mid, n - 1, jnp.where(n == 0, g, 2 + g))

    def direct_copy(n, o):
        to = at_win(o)
        return pltpu.make_async_remote_copy(
            packed.at[n, lax.rem(to, 4), pl.ds(pl.multiple_of((to // 4) * 64, 64), 64)],
            direct_in.at[n, o - 1], direct_send.at[n, o - 1], direct_recv.at[n, o - 1],
            device_id=(sta, to), device_id_type=MESH,
        )

    def lin(v):
        return v * jnp.abs(v) * (1.0 / (LIN_CODE * LIN_CODE))

    def wide(v):
        return v.astype(jnp.int32).astype(F32)

    def added(vs):
        while len(vs) > 1:
            vs = [sum(vs[i : i + 2]) for i in range(0, len(vs), 2)]
        return vs[0]

    def decoded(read):
        first = added([lin(wide(v)) for v in read(0, 16)])
        rest = added([wide(v) for v in read(16, 32)]) * (1.0 / PHASE_CODE)
        end = [wide(v) for v in read(48, 16)]
        end = added([jnp.where(lanes((16, 128)) < 4, lin(v), v * (1.0 / PHASE_CODE)) for v in end])
        return first, rest, end[0:8]

    def count_copy(o):
        return pltpu.make_async_remote_copy(
            counts, counts_in.at[o - 1], count_send.at[o - 1], count_recv.at[o - 1],
            device_id=(sta, at_win(o)), device_id_type=MESH,
        )

    def weighted(lin, pr, pi, inv):
        pr, pi = pr * inv, pi * inv
        return lin * inv * (pr * pr + pi * pi)

    def mir_copy(n, g, which, src=stack):
        dst, to = ((mirror, flip), (mirror2, turn))[which]
        return pltpu.make_async_remote_copy(
            src.at[n, g], dst.at[n - 1, g], mir_send.at[n - 1, 2 * g + which], mir_recv.at[n - 1, 2 * g + which],
            device_id=(at_sta(1 + g), to), device_id_type=MESH,
        )

    def finish(n):
        for o in range(1, WIN):
            direct_copy(n, o).wait_recv()

        def read(row, size):
            at = pl.ds(pl.multiple_of(high * 64 + row, 16), size)
            vs = [packed[pl.ds(n, 1), pl.ds(level, 1), at, :][0, 0]]
            return vs + [direct_in[pl.ds(n, 1), o, row : row + size, :][0] for o in range(7)]

        conclude(n, jnp.concatenate(decoded(read), axis=0))

    def conclude(n, v):
        for g in (0, 1):
            rows = [v[16 * q + 8 * g : 16 * q + 8 * g + 8] for q in range(3)]
            stack[pl.ds(n, 1), g] = weighted(*rows, inverse[pl.ds(n, 1), g][0])[None]

        @pl.when((n > 0) & (n < 5))
        def _():
            for g in (0, 1):
                mir_copy(n, g, 0).start()

            @pl.when(win != 0)
            def _():
                for g in (0, 1):
                    mir_copy(n, g, 1).start()

            @pl.when(win == 0)
            def _():
                e = v[48:56]
                end = weighted(e, pltpu.roll(e, 124, 1), pltpu.roll(e, 120, 1), inverse_end[pl.ds(n, 1)][0])
                for g in (0, 1):
                    t = stack[pl.ds(n, 1), g][0]
                    for h in (0, 1):
                        t = jnp.where(lane == 63 + 64 * h, end[:, 2 * g + h : 2 * g + h + 1], t)
                    stack2[pl.ds(n, 1), g] = t[None]
                    mir_copy(n, g, 1, stack2).start()

    def send(n):
        for o in range(1, WIN):
            direct_copy(n, o).start()

    def arrive(k, jj):
        @pl.when(k == 1)
        def _():
            for h in (0, 1):
                up_copy(2 * jj + h).wait_recv()

                @pl.when(odd)
                def _():
                    pass_copy(2 * jj + h).start()

        @pl.when(k == 2)
        def _():
            for h in (0, 1):
                two_copy(2 * jj + h).wait_recv()

    def settle():
        heard(2)
        v = counts[...]
        for o in range(1, WIN):
            count_copy(o).wait_recv()
            v = v + counts_in[o - 1]
        v = 1.0 / jnp.maximum(v, 1.0)
        for m in range(6):
            end = jnp.ones((8, 128), F32)
            for g in (0, 1):
                k, jj = (1 + g, m - 1) if 0 < m < 5 else (0, g + (2 if m else 0))
                two = [v[:, k * 8 + 2 * jj + h : k * 8 + 2 * jj + h + 1] for h in (0, 1)]
                inverse[m, g] = jnp.where(low, *two)
                for h in (0, 1):
                    end = jnp.where(lane == 2 * g + h, two[h], end)
            inverse_end[m] = end

    def step(n, carry):
        k, jj = pair_of(n, 1)
        arrive(k, jj)
        post(0)
        cross(k, jj)
        product()
        k, jj = pair_of(n + 1, 0)
        arrive(k, jj)
        post(1)
        cross(k, jj)
        product()
        encode(n)

        @pl.when(n == 0)
        def _():
            heard(0)
            tell(1)

        @pl.when(n == 1)
        def _():
            heard(1)
            tell(2)
            send(0)

        @pl.when(n >= 1)
        def _():
            send(n)

        @pl.when(n == 1)
        def _():
            for m in (1, 2):
                flag_copy(m).wait_recv()
                all_flags[8 * m : 8 * m + 8, :] = flags_in[m - 1]
            counts[...] = lax.dot_general(
                flags[...].astype(BF), all_flags[...].astype(BF), (((1,), (1,)), ((), ())), preferred_element_type=F32
            )
            for o in range(1, WIN):
                count_copy(o).start()

        return carry

    cross(0, 0)
    product()
    lax.fori_loop(0, 4, step, 0)
    arrive(2, 3)
    post(0)
    cross(2, 3)
    product()
    post(1)
    encode(4)
    send(4)
    cross(0, 2)
    product()
    settle()
    for n in range(3):
        finish(n)
    post(0)
    cross(0, 3)
    product()
    finish(3)
    post(1)
    encode(5)
    send(5)
    finish(4)
    row_id = lax.broadcasted_iota(jnp.int32, (128, 128), 0)
    col_id = lanes((128, 128))
    side, place = col_id // 64, lax.rem(col_id, 64)
    lower = win < 4
    take = side * 64 + jnp.where(lower, 63 - place, place)
    direct = jnp.where(row_id == take, 1.0, 0.0)
    take = side * 64 + jnp.where(lower, 64 - place, place - 1)
    mirrored = jnp.where((row_id == take) & (place != 0), 1.0, 0.0)
    take = side * 64 + jnp.where(turn < 4, 63, 0)
    ending = jnp.where((row_id == take) & (place == 0), 1.0, 0.0)

    def ordered(v, table):
        return jnp.dot(v, table, precision=lax.Precision.HIGHEST, preferred_element_type=F32)

    keep_all[...] = jnp.zeros_like(keep_all)
    for k in range(5):
        keep_all[:, 8 * k : 8 * k + 8] = keep_in[k].astype(F32)
    keep = keep_all[...]
    masks = []
    for n in range(8):
        k, jj = 1 + n % 2, n // 2
        spot = lane == (2 - k) * 8 + lax.broadcasted_iota(jnp.int32, (8, 128), 0)
        masks.append(jnp.where(low, *[
            jnp.sum(jnp.where(spot, keep[j : j + 1, :], 0.0), axis=1, keepdims=True) for j in (2 * jj, 2 * jj + 1)
        ]))
    finish(5)

    v = ordered(stack[...].reshape(96, 128), direct)
    for d in range(12):
        n, g = d // 2, d % 2
        k, jj = (1 + g, n - 1) if 0 < n < 5 else (0, g + (2 if n else 0))
        t = v[8 * d : 8 * d + 8]
        at = (k + 2) * 8 + 2 * jj
        t = t * jnp.where(low, keep[:, at : at + 1], keep[:, at + 1 : at + 2])
        out_ref[pl.ds(at, 8, stride=40), :] = t
        out_ref[pl.ds(at + 1, 8, stride=40), :] = pltpu.roll(t, 64, 1)

    for d in (1, 2):
        flag_copy(d).wait_send()
    for j in range(8):
        up_copy(j).wait_send()

    @pl.when(odd)
    def _():
        for j in range(8):
            two_copy(j).wait_send()
            pass_copy(j).wait_send()

    for o in range(1, WIN):
        count_copy(o).wait_send()

    def drain(n, carry):
        for o in range(1, WIN):
            direct_copy(n, o).wait_send()
        return carry

    lax.fori_loop(0, 6, drain, 0)
    for n in range(1, 5):
        for g in (0, 1):
            for which in (0, 1):
                mir_copy(n, g, which).wait_recv()
    v = ordered(mirror[...].reshape(64, 128), mirrored) + ordered(mirror2[...].reshape(64, 128), ending)
    for n in range(8):
        k, jj = 1 + n % 2, n // 2
        t = v[8 * n : 8 * n + 8]
        at = 2 * jj * 40 + (2 - k) * 8
        t = t * masks[n]
        out_ref[at : at + 8, :] = t
        out_ref[at + 40 : at + 48, :] = pltpu.roll(t, 64, 1)

    for n in range(1, 5):
        for g in (0, 1):
            for which in (0, 1):
                mir_copy(n, g, which).wait_send()


def local(n_sta, traces, gap_mask, pair_mask):
    vmem, dma = pltpu.VMEM, pltpu.SemaphoreType.DMA
    anywhere = pl.BlockSpec(memory_space=pltpu.HBM)
    inside = pl.BlockSpec(memory_space=pltpu.VMEM)
    stacked = pl.pallas_call(
        functools.partial(kernel, n_sta),
        out_shape=jax.ShapeDtypeStruct((320, 128), F32),
        in_specs=[anywhere] * 5,
        out_specs=inside,
        scratch_shapes=[
            vmem((8, 16), jnp.int32),
            vmem((5, 8, 8), jnp.int32),
            vmem((128, 2048), F32),
            vmem((768, 2048), BF),
            vmem((1024, 512), BF),
            vmem((1024, 256), BF),
            vmem((512, 512), F32),
            vmem((512, 512), F32),
            vmem((256, 512), F32),
            vmem((128, 256), F32),
            vmem((128, 256), F32),
            vmem((3, 8, 16, 2048), BF),
            vmem((16, 128, 128), F32),
            vmem((2, 16, 2048), F32),
            vmem((512, 1024), BF),
            vmem((512, 512), F32),
            vmem((4, 128, 128), F32),
            vmem((8, 128), F32),
            vmem((2, 8, 128), F32),
            vmem((8, 128), F32),
            vmem((128, 128), F32),
            vmem((8, 128), F32),
            vmem((7, 8, 128), F32),
            vmem((6, 2, 8, 128), F32),
            vmem((6, 8, 128), F32),
            vmem((8, 48, 128), F32),
            vmem((8, 128), F32),
            vmem((6, 4, 128, 128), jnp.int16),
            vmem((6, 7, 64, 128), jnp.int16),
            vmem((6, 2, 8, 128), F32),
            vmem((6, 2, 8, 128), F32),
            vmem((4, 2, 8, 128), F32),
            vmem((4, 2, 8, 128), F32),
            pltpu.SemaphoreType.REGULAR((3,)),
            dma((5,)),
            dma((2,)),
            dma((2,)),
            dma((8,)),
            dma((8,)),
            dma((8,)),
            dma((2, 8)),
            dma((7,)),
            dma((7,)),
            dma((6, 7)),
            dma((6, 7)),
            dma((4, 4)),
            dma((4, 4)),
        ],
        compiler_params=pltpu.CompilerParams(
            collective_id=0, has_side_effects=True, vmem_limit_bytes=66600000,
        ),
    )(traces.reshape(128, SAMPLES), gap_mask, jnp.transpose(pair_mask, (1, 0, 2)), jnp.asarray(forward_table()), jnp.asarray(inverse_table()))
    return stacked.reshape(8, 5, 8, 128)[..., :64]


def solution(mesh):
    return jax.shard_map(
        functools.partial(local, mesh.shape["sta"]),
        mesh=mesh,
        in_specs=(P("sta", "win", None), P("sta", "win"), P("sta", None, None)),
        out_specs=P("sta", None, None, "win"),
        check_vma=False,
    )
```
